128 devices in a mesh: samp: 32 (over x, y, core), var: 4 (over z).
Axes of the slice: x: 4, y: 4, z: 4, core: 2. Of those that a mesh axis runs over, the one named last changes fastest.
Arguments:
- genotypes: int32 [32768, 4096], P('samp', 'var'), may hold values from 0 to 2
- observed: int32 [32768, 4096], P('samp', 'var'), may hold values from 0 to 1, as said below
- proportions: float32 [10, 32768], P(None, 'samp'), may hold values from 0 to 1, as said below
- frequencies: float32 [10, 4096], P(None, ('samp', 'var')), may hold values from 0.02 to 0.98
Outputs:
- mixture: float32 [10, 32768], P(None, 'samp')
- alleles: float32 [10, 4096], P(None, 'var')
The draws below stay inside these ranges and needn't reach their ends.
Inputs may be any that keep to these rules, and one draw needn't show every extreme that they name: Every sample is observed at 256 or more variants and every variant at 2048 or more samples. Each sample's 10 proportions are positive and sum to one.
All inputs are finite; a program needn't handle non-finite values.
Results may differ from the reference program's by a relative error of at most 0.0003.
Values sent between devices are 32-bit elements; how exact they have to be, the bound alone decides.
A program may use at most 128 MiB of HBM per device.

```python
import jax
import jax.numpy as jnp
from jax import lax

K = 10
N_DEV = 1024
STEPS = 2
SAMPLES = 32768
M = 4096


def draw_observed(key, part):
    key_cells, key_rows, key_cols = jax.random.split(jax.random.fold_in(key, 11), 3)
    missing_draw = jax.random.randint(key_cells, (SAMPLES, M), 0, 16)
    row_shift = jax.random.randint(key_rows, (SAMPLES, 1), 0, 16)
    col_shift = jax.random.randint(key_cols, (1, M), 0, 16)
    row_index = lax.broadcasted_iota(jnp.int32, (SAMPLES, 1), 0)
    col_index = lax.broadcasted_iota(jnp.int32, (1, M), 1)
    kept = (missing_draw != 0) | ((col_index + row_shift) % 16 == 0) | ((row_index + col_shift) % 16 == 0)
    return kept.astype(jnp.int32)


def draw_proportions(key, part):
    inner = jax.random.fold_in(key, 23)
    raw_logs = jax.random.uniform(inner, (K, SAMPLES), jnp.float32, -2.0, 2.0)
    weights = jnp.exp(raw_logs)
    return weights / jnp.sum(weights, axis=0, keepdims=True)


def touch_ends(entries, rng, smallest, top_value):
    dims = entries.shape
    spot = [jax.random.randint(jax.random.fold_in(rng, axis), (), 0, dims[axis]) for axis in range(len(dims))]
    entries = entries.at[tuple(spot)].set(smallest)
    longest = dims.index(max(dims))
    spot[longest] = (spot[longest] + 1) % dims[longest]
    return entries.at[tuple(spot)].set(top_value)


def level_of(own_key, shape, cuts, low, high):
    def one(position, shards_of):
        draws = jax.random.uniform(jax.random.fold_in(jax.random.fold_in(own_key, 6), position), (shards_of,), jnp.float32, low / len(cuts), high / len(cuts))
        return jnp.repeat(jnp.exp(draws), shape[position] // shards_of).reshape((-1,) + (1,) * (len(shape) - position - 1))

    gain = one(*cuts[0])
    for cut in cuts[1:]:
        gain = gain * one(*cut)
    return gain


def setup_inputs(seed: int = 0) -> dict:
    key_list = jax.random.split(jax.random.key(seed), 5)
    genotypes = touch_ends(jax.random.randint(key_list[0], (SAMPLES, M), 0, 3), jax.random.fold_in(key_list[0], 1), 0, 2).astype(jnp.int32)
    observed = draw_observed(jax.random.fold_in(key_list[4], 71), 0)
    proportions = draw_proportions(jax.random.fold_in(key_list[4], 71), 0)
    frequencies = jnp.clip(0.02 + 0.96000002 * jax.random.uniform(key_list[3], (K, M), jnp.float32) ** level_of(key_list[3], (K, M), ((1, 128),), -0.2, 0.2), 0.02, 0.98)
    return dict(genotypes=genotypes, observed=observed, proportions=proportions, frequencies=frequencies)


CLIP_LOW = 1e-05
NORM_EPS = 1e-10
EXACT = lax.Precision.HIGHEST

def clip_unit(values):
    return jnp.clip(values, CLIP_LOW, 1.0 - CLIP_LOW)

def tidy_mixture(mixture):
    clipped = clip_unit(mixture)
    return clipped / lax.optimization_barrier(jnp.sum(clipped, axis=0, keepdims=True))

def step_size(first, second):
    return jnp.maximum(1.0, jnp.sqrt(first / (second + NORM_EPS)))

def expectation_step(genotypes, observed, twice_observed, mixture, alleles):
    block_count = SAMPLES // N_DEV
    geno_blocks = genotypes.reshape(block_count, N_DEV, M)
    seen_blocks = observed.reshape(block_count, N_DEV, M)
    mix_blocks = jnp.transpose(mixture.reshape(K, block_count, N_DEV), (1, 0, 2))

    def visit_block(running, block_data):
        geno_block, seen_block, mix_block = block_data
        geno_vals = geno_block.astype(jnp.float32)
        seen_vals = seen_block.astype(jnp.float32)
        expected = lax.dot_general(mix_block, alleles, (((0,), (0,)), ((), ())), precision=EXACT, preferred_element_type=jnp.float32)
        ratio_alt = seen_vals * geno_vals / expected
        ratio_ref = seen_vals * (2.0 - geno_vals) / (1.0 - expected)
        prop_terms = lax.dot_general(alleles, ratio_alt, (((1,), (1,)), ((), ())), precision=EXACT, preferred_element_type=jnp.float32)
        prop_terms = prop_terms + lax.dot_general(1.0 - alleles, ratio_ref, (((1,), (1,)), ((), ())), precision=EXACT, preferred_element_type=jnp.float32)
        alt_terms = lax.dot_general(mix_block, ratio_alt, (((1,), (0,)), ((), ())), precision=EXACT, preferred_element_type=jnp.float32)
        ref_terms = lax.dot_general(mix_block, ratio_ref, (((1,), (0,)), ((), ())), precision=EXACT, preferred_element_type=jnp.float32)
        return ((running[0] + alt_terms, running[1] + ref_terms), prop_terms)
    zeros_start = jnp.zeros((K, M), jnp.float32)
    sums_pair, prop_blocks = lax.scan(visit_block, (zeros_start, zeros_start), (geno_blocks, seen_blocks, mix_blocks))
    alt_sums, ref_sums = sums_pair
    prop_sums = jnp.transpose(prop_blocks, (1, 0, 2)).reshape(K, SAMPLES)
    next_mixture = clip_unit(mixture * prop_sums / twice_observed)
    weighted = alleles * alt_sums
    next_alleles = clip_unit(weighted / (weighted + (1.0 - alleles) * ref_sums))
    return (next_mixture, next_alleles)

def reference(genotypes, observed, proportions, frequencies):
    twice_observed = 2.0 * lax.optimization_barrier(jnp.sum(observed, axis=1)).astype(jnp.float32)[None, :]
    mixture, alleles = (proportions, frequencies)
    for repeat in range(STEPS):
        mixture_one, alleles_one = expectation_step(genotypes, observed, twice_observed, mixture, alleles)
        mixture_two, alleles_two = expectation_step(genotypes, observed, twice_observed, mixture_one, alleles_one)
        step_mix = mixture_one - mixture
        curve_mix = mixture_two - mixture_one - step_mix
        step_allele = alleles_one - alleles
        curve_allele = alleles_two - alleles_one - step_allele
        alpha_mix = step_size(jnp.sum(step_mix * step_mix), jnp.sum(curve_mix * curve_mix))
        alpha_allele = step_size(jnp.sum(step_allele * step_allele), jnp.sum(curve_allele * curve_allele))
        extra_mix = tidy_mixture(mixture + 2.0 * alpha_mix * step_mix + alpha_mix * alpha_mix * curve_mix)
        extra_allele = clip_unit(alleles + 2.0 * alpha_allele * step_allele + alpha_allele * alpha_allele * curve_allele)
        mixture, alleles = expectation_step(genotypes, observed, twice_observed, extra_mix, extra_allele)
    return (mixture, alleles)
```

```python
import functools

import jax
import jax.numpy as jnp
from jax import lax
from jax.experimental import pallas as pl
from jax.experimental.pallas import tpu as pltpu
from jax.sharding import PartitionSpec as P

STEPS = 2
CLIP_LOW = 1e-05
NORM_EPS = 1e-10
MESH = pl.DeviceIdType.MESH

K = 10
ROWS = 16
NS = 32
NV = 4
SAMP = 1024
VARS = 1024
LANES = 128
TILES = VARS // LANES
PIECES = 24
RB = 256
CB = 256
CHUNK = 128
CHUNKS = SAMP // CHUNK

F32 = jnp.float32
BF16 = jnp.bfloat16


def clip_unit(values):
    return jnp.clip(values, CLIP_LOW, 1.0 - CLIP_LOW)


def split3(values):
    high = values.astype(BF16).astype(F32)
    rest = values - high
    mid = rest.astype(BF16).astype(F32)
    low = (rest - mid).astype(BF16).astype(F32)
    return high, mid, low


def split2(values):
    high = values.astype(BF16)
    low = (values - high.astype(F32)).astype(BF16)
    return high, low


def dot(a, b):
    return lax.dot_general(
        a, b, (((1,), (0,)), ((), ())), preferred_element_type=F32
    )


def owner_of(piece):
    return lax.rem(piece, 16) * 2 + piece // 16


def kernel(
    geno_hbm,
    seen_hbm,
    props_ref,
    freqs_ref,
    mix_ref,
    allele_ref,
    geno_buf,
    seen_buf,
    alt_cnt,
    ref_cnt,
    count_acc,
    prop_acc,
    q_now,
    q_start,
    q_one,
    p_now,
    p_start,
    p_one,
    q_cols,
    p_rows,
    q_rows,
    p_cols,
    f_send,
    f_recv,
    tile_all,
    rs_send,
    rs_recv,
    ag_all,
    z_all,
    sq_q,
    sq_p,
    load_sem,
    f_sems,
    t_sems,
    rs_sems,
    ag_sems,
    z_send,
    z_recv,
    sq_sems,
    sp_sems,
):
    s = lax.axis_index("samp")
    v = lax.axis_index("var")
    my_piece = lax.rem(s, 2) * 16 + s // 2
    is_owner = my_piece < PIECES
    my_q = my_piece // TILES
    my_t = lax.rem(my_piece, TILES)
    home = s // TILES
    tile_here = home == v
    t_first = v * TILES

    def remote(src, dst, send_sem, recv_sem, where):
        return pltpu.make_async_remote_copy(
            src_ref=src,
            dst_ref=dst,
            send_sem=send_sem,
            recv_sem=recv_sem,
            device_id=where,
            device_id_type=MESH,
        )

    def wait_bytes(ref, sem):
        pltpu.make_async_copy(ref, ref, sem).wait()

    def load(chunk):
        rows = pl.ds(chunk * CHUNK, CHUNK)
        return (
            pltpu.make_async_copy(geno_hbm.at[rows], geno_buf.at[rows], load_sem.at[0, chunk]),
            pltpu.make_async_copy(seen_hbm.at[rows], seen_buf.at[rows], load_sem.at[1, chunk]),
        )

    for chunk in range(CHUNKS):
        for copy in load(chunk):
            copy.start()

    barrier = pltpu.get_barrier_semaphore()

    def greet_samp(d, carry):
        pl.semaphore_signal(barrier, inc=1, device_id=(lax.rem(s + d, NS), v), device_id_type=MESH)
        return carry

    def greet_var(d, carry):
        pl.semaphore_signal(barrier, inc=1, device_id=(s, lax.rem(v + d, NV)), device_id_type=MESH)
        return carry

    lax.fori_loop(1, NV, greet_var, 0)
    lax.fori_loop(1, NS, greet_samp, 0)

    row_ids = lax.broadcasted_iota(jnp.int32, (ROWS, 1), 0)
    row_mask = row_ids < K

    block = jnp.concatenate([freqs_ref[...], jnp.zeros((ROWS - K, 32), F32)], axis=0)
    block = jnp.concatenate([block, block, block, block], axis=1)
    lane_group = lax.broadcasted_iota(jnp.int32, (ROWS, LANES), 1) // 32
    block = jnp.where(lane_group == v, block, 0.0)
    f_send[...] = block
    q_now[...] = jnp.concatenate([props_ref[...], jnp.zeros((ROWS - K, SAMP), F32)], axis=0)

    pl.semaphore_wait(barrier, NS - 1 + NV - 1)

    @pl.when(jnp.logical_not(tile_here))
    def _():
        remote(f_send, f_recv.at[v], f_sems.at[0], f_sems.at[1], (s, home)).start()

    lane_ids = lax.broadcasted_iota(jnp.int32, (VARS, LANES), 1)
    count_w = jnp.where(lane_ids == 3 * ROWS + K, 2.0, 0.0).astype(BF16)

    def convert(chunk):
        for copy in load(chunk):
            copy.wait()
        rows = pl.ds(chunk * CHUNK, CHUNK)
        seen = seen_buf[rows, :].astype(F32)
        alt = seen * geno_buf[rows, :].astype(F32)
        alt_cnt[rows, :] = alt
        ref_cnt[rows, :] = 2.0 * seen - alt
        count_acc[rows, :] = dot(seen.astype(BF16), count_w)

    for chunk in range(CHUNKS // 2):
        convert(chunk)

    @pl.when(tile_here)
    def _():
        wait_bytes(f_recv.at[pl.ds(0, NV - 1)], f_sems.at[1])
        f_recv[v] = block
        tile = f_recv[0] + f_recv[1] + f_recv[2] + f_recv[3]
        tile_all[lax.rem(s, TILES)] = tile

        def send_tile(d, carry):
            slot = tile_all.at[lax.rem(s, TILES)]
            remote(slot, slot, t_sems.at[0], t_sems.at[1], (lax.rem(s + d, NS), v)).start()
            return carry

        lax.fori_loop(1, NS, send_tile, 0)

    for chunk in range(CHUNKS // 2, CHUNKS):
        convert(chunk)

    @pl.when(tile_here)
    def _():
        wait_bytes(tile_all.at[pl.ds(0, TILES - 1)], t_sems.at[1])

    @pl.when(jnp.logical_not(tile_here))
    def _():
        wait_bytes(tile_all, t_sems.at[1])
        remote(f_send, f_recv.at[v], f_sems.at[0], f_sems.at[1], (s, home)).wait_send()

    @pl.when(tile_here)
    def _():
        slot = tile_all.at[0]

        def drain(d, carry):
            wait_bytes(slot, t_sems.at[0])
            return carry

        lax.fori_loop(1, NS, drain, 0)

    for t in range(TILES):
        p_now[t] = tile_all[t]

    def full_p(ref):
        return jnp.concatenate([ref[t] for t in range(TILES)], axis=1)

    def em_step(step, carry):
        phase = lax.rem(step, 3)
        parity = lax.rem(step, 2)
        q = q_now[...]
        p = full_p(p_now)
        qh, qm, ql = split3(q)
        ph, pm, pL = split3(p)
        pad = jnp.zeros((2 * ROWS, SAMP), F32)
        pad5 = jnp.zeros((5 * ROWS, SAMP), F32)
        q_cols[...] = jnp.concatenate([qh, qh, qm, qm, qh, ql, pad], axis=0).T.astype(BF16)
        p_rows[...] = jnp.concatenate([ph, pm, ph, pm, pL, ph, pad], axis=0).astype(BF16)
        q_rows[...] = jnp.concatenate([qh, qm, ql], axis=0).astype(BF16)
        p_cols[...] = jnp.concatenate([ph, pm, pL, pad5], axis=0).T.astype(BF16)

        for cb in range(VARS // CB):
            cols = pl.ds(cb * CB, CB)
            p_part = p_rows[:, cols]
            p_weights = p_cols[cols, :]

            def row_block(rb, sums):
                alt_sum, ref_sum = sums
                rows = pl.ds(pl.multiple_of(rb * RB, RB), RB)
                expected = dot(q_cols[rows, :], p_part)
                other = 1.0 - expected
                inverse = 1.0 / (expected * other)
                ratio_alt = alt_cnt[rows, cols] * (other * inverse)
                ratio_ref = ref_cnt[rows, cols] * (expected * inverse)
                alt_high, alt_low = split2(ratio_alt)
                ref_high, ref_low = split2(ratio_ref)
                diff_high, diff_low = split2(ratio_alt - ratio_ref)
                q_part = q_rows[:, rows]
                alt_sum = alt_sum + (dot(q_part, alt_high) + dot(q_part, alt_low))
                ref_sum = ref_sum + (dot(q_part, ref_high) + dot(q_part, ref_low))
                before = count_acc[rows, :] if cb == 0 else prop_acc[rows, :]
                prop_acc[rows, :] = before + (dot(diff_high, p_weights) + dot(diff_low, p_weights))
                return alt_sum, ref_sum

            zero = jnp.zeros((3 * ROWS, CB), F32)
            alt3, ref3 = zero, zero
            for rb in range(SAMP // RB):
                alt3, ref3 = row_block(rb, (alt3, ref3))
            alt = alt3[:ROWS] + alt3[ROWS : 2 * ROWS] + alt3[2 * ROWS :]
            ref = ref3[:ROWS] + ref3[ROWS : 2 * ROWS] + ref3[2 * ROWS :]
            for t in range(cb * CB // LANES, (cb + 1) * CB // LANES):
                lane = t * LANES - cb * CB
                for part in range(3):
                    piece = part * TILES + t
                    target = (piece % 16) * 2 + piece // 16
                    rs_send[piece] = jnp.concatenate(
                        [
                            alt[4 * part : 4 * part + 4, lane : lane + LANES],
                            ref[4 * part : 4 * part + 4, lane : lane + LANES],
                        ],
                        axis=0,
                    )

                    @pl.when(s != target)
                    def _():
                        remote(
                            rs_send.at[piece],
                            rs_recv.at[s],
                            rs_sems.at[0],
                            rs_sems.at[1],
                            (target, v),
                        ).start()

        turned = prop_acc[...].T
        z_all[parity, v] = (
            turned[:ROWS]
            + turned[ROWS : 2 * ROWS]
            + turned[2 * ROWS : 3 * ROWS]
            + turned[3 * ROWS : 4 * ROWS]
        )

        def send_z(d, carry):
            slot = z_all.at[parity, v]
            remote(slot, slot, z_send.at[0], z_recv.at[parity], (s, lax.rem(v + d, NV))).start()
            return carry

        lax.fori_loop(1, NV, send_z, 0)

        wait_bytes(z_all.at[parity, pl.ds(0, NV - 1)], z_recv.at[parity])
        total = z_all[parity, 0] + z_all[parity, 1] + z_all[parity, 2] + z_all[parity, 3]
        twice = total[K : K + 1, :]
        inner = jnp.sum(q * total, axis=0, keepdims=True)
        q_next = jnp.where(row_mask, clip_unit(q * (1.0 + (total - inner) / twice)), 0.0)

        @pl.when(phase == 1)
        def _():
            step_mix = q_one[...] - q_start[...]
            curve_mix = q_next - q_one[...] - step_mix
            row = [jnp.sum(a * a, axis=0, keepdims=True) for a in (step_mix, curve_mix)]
            row = jnp.concatenate(row, axis=0)
            part = row[:, :LANES]
            for t in range(1, TILES):
                part = part + row[:, t * LANES : (t + 1) * LANES]
            sq_q[s] = part

            def send_sq(d, carry):
                slot = sq_q.at[s]
                remote(slot, slot, sq_sems.at[0], sq_sems.at[1], (lax.rem(s + d, NS), v)).start()
                return carry

            lax.fori_loop(1, NS, send_sq, 0)

        @pl.when(is_owner)
        def _():
            wait_bytes(rs_recv.at[pl.ds(0, NS - 1)], rs_sems.at[1])
            rs_recv[s] = rs_send[my_piece]
            sums = [rs_recv[i] for i in range(NS)]
            while len(sums) > 1:
                sums = [sums[i] + sums[i + 1] for i in range(0, len(sums), 2)]
            alt_sum, ref_sum = sums[0][:4], sums[0][4:]
            tile = p_now[my_t]
            old = jnp.where(my_q == 0, tile[:4], jnp.where(my_q == 1, tile[4:8], tile[8:12]))
            weighted = old * alt_sum
            new = clip_unit(weighted / (weighted + (1.0 - old) * ref_sum))
            piece_row = 4 * my_q + lax.broadcasted_iota(jnp.int32, (4, LANES), 0)
            ag_all[my_piece] = jnp.where(piece_row < K, new, 0.0)

            def send_ag(d, carry):
                slot = ag_all.at[my_piece]
                remote(slot, slot, ag_sems.at[0], ag_sems.at[1], (lax.rem(s + d, NS), v)).start()
                return carry

            lax.fori_loop(1, NS, send_ag, 0)
            wait_bytes(ag_all.at[pl.ds(0, PIECES - 1)], ag_sems.at[1])

        @pl.when(jnp.logical_not(is_owner))
        def _():
            wait_bytes(ag_all, ag_sems.at[1])

        zeros4 = jnp.zeros((4, LANES), F32)
        p_next = [
            jnp.concatenate([ag_all[t], ag_all[TILES + t], ag_all[2 * TILES + t], zeros4], axis=0)
            for t in range(TILES)
        ]

        @pl.when(phase == 0)
        def _():
            q_start[...] = q
            q_one[...] = q_next
            q_now[...] = q_next
            for t in range(TILES):
                p_start[t] = p_now[t]
                p_one[t] = p_next[t]
                p_now[t] = p_next[t]

        @pl.when(phase == 2)
        def _():
            q_now[...] = q_next
            for t in range(TILES):
                p_now[t] = p_next[t]

        @pl.when(phase == 1)
        def _():
            part_r = jnp.zeros((ROWS, LANES), F32)
            part_v = jnp.zeros((ROWS, LANES), F32)
            for t in range(TILES):
                r = p_one[t] - p_start[t]
                c = p_next[t] - p_one[t] - r
                part_r = part_r + r * r
                part_v = part_v + c * c
            sq_p[v] = jnp.concatenate(
                [jnp.sum(part_r, axis=0, keepdims=True), jnp.sum(part_v, axis=0, keepdims=True)],
                axis=0,
            )

            def send_sp(d, carry):
                slot = sq_p.at[v]
                remote(slot, slot, sp_sems.at[0], sp_sems.at[1], (s, lax.rem(v + d, NV))).start()
                return carry

            lax.fori_loop(1, NV, send_sp, 0)

            def alpha_of(sums):
                first = jnp.sum(sums[0:1], axis=1, keepdims=True)
                second = jnp.sum(sums[1:2], axis=1, keepdims=True)
                return jnp.maximum(1.0, jnp.sqrt(first / (second + NORM_EPS)))

            wait_bytes(sq_q.at[pl.ds(0, NS - 1)], sq_sems.at[1])
            sums = [sq_q[i] for i in range(NS)]
            while len(sums) > 1:
                sums = [sums[i] + sums[i + 1] for i in range(0, len(sums), 2)]
            alpha = alpha_of(sums[0])
            base = q_start[...]
            step_mix = q_one[...] - base
            curve_mix = q_next - q_one[...] - step_mix
            extra = clip_unit(base + 2.0 * alpha * step_mix + alpha * alpha * curve_mix)
            extra = jnp.where(row_mask, extra, 0.0)
            q_now[...] = extra / jnp.sum(extra, axis=0, keepdims=True)

            wait_bytes(sq_p.at[pl.ds(0, NV - 1)], sp_sems.at[1])
            alpha_p = alpha_of(sq_p[0] + sq_p[1] + sq_p[2] + sq_p[3])
            for t in range(TILES):
                base_p = p_start[t]
                r = p_one[t] - base_p
                c = p_next[t] - p_one[t] - r
                extra_p = clip_unit(base_p + 2.0 * alpha_p * r + alpha_p * alpha_p * c)
                p_now[t] = jnp.where(row_mask, extra_p, 0.0)

            wait_bytes(sq_q.at[pl.ds(0, NS - 1)], sq_sems.at[0])
            wait_bytes(sq_p.at[pl.ds(0, NV - 1)], sp_sems.at[0])

        wait_bytes(z_all.at[parity, pl.ds(0, NV - 1)], z_send.at[0])
        wait_bytes(rs_send.at[pl.ds(0, PIECES - 1)], rs_sems.at[0])

        @pl.when(is_owner)
        def _():
            wait_bytes(ag_all, ag_sems.at[0])
            wait_bytes(ag_all.at[pl.ds(0, NS - 1 - PIECES)], ag_sems.at[0])

        @pl.when(jnp.logical_not(is_owner))
        def _():
            wait_bytes(rs_send.at[0], rs_sems.at[0])

        return carry

    lax.fori_loop(0, 3 * STEPS, em_step, 0)
    mix_ref[...] = q_now[:K, :]
    for t in range(TILES):
        allele_ref[:, t * LANES : (t + 1) * LANES] = p_now[t][:K]


def local(genotypes, observed, proportions, frequencies):
    vmem = pl.BlockSpec(memory_space=pltpu.VMEM)
    hbm = pl.BlockSpec(memory_space=pl.ANY)
    dma = pltpu.SemaphoreType.DMA
    return pl.pallas_call(
        kernel,
        name="em",
        out_shape=(
            jax.ShapeDtypeStruct((K, SAMP), F32),
            jax.ShapeDtypeStruct((K, VARS), F32),
        ),
        in_specs=[hbm, hbm, vmem, vmem],
        out_specs=(vmem, vmem),
        scratch_shapes=[
            pltpu.VMEM((SAMP, VARS), jnp.int32),
            pltpu.VMEM((SAMP, VARS), jnp.int32),
            pltpu.VMEM((SAMP, VARS), F32),
            pltpu.VMEM((SAMP, VARS), F32),
            pltpu.VMEM((SAMP, LANES), F32),
            pltpu.VMEM((SAMP, LANES), F32),
            pltpu.VMEM((ROWS, SAMP), F32),
            pltpu.VMEM((ROWS, SAMP), F32),
            pltpu.VMEM((ROWS, SAMP), F32),
            pltpu.VMEM((TILES, ROWS, LANES), F32),
            pltpu.VMEM((TILES, ROWS, LANES), F32),
            pltpu.VMEM((TILES, ROWS, LANES), F32),
            pltpu.VMEM((SAMP, LANES), BF16),
            pltpu.VMEM((LANES, VARS), BF16),
            pltpu.VMEM((3 * ROWS, SAMP), BF16),
            pltpu.VMEM((VARS, LANES), BF16),
            pltpu.VMEM((ROWS, LANES), F32),
            pltpu.VMEM((NV, ROWS, LANES), F32),
            pltpu.VMEM((TILES, ROWS, LANES), F32),
            pltpu.VMEM((PIECES, 8, LANES), F32),
            pltpu.VMEM((NS, 8, LANES), F32),
            pltpu.VMEM((PIECES, 4, LANES), F32),
            pltpu.VMEM((2, NV, ROWS, SAMP), F32),
            pltpu.VMEM((NS, 2, LANES), F32),
            pltpu.VMEM((NV, 2, LANES), F32),
            dma((2, CHUNKS)),
            dma((2,)),
            dma((2,)),
            dma((2,)),
            dma((2,)),
            dma((1,)),
            dma((2,)),
            dma((2,)),
            dma((2,)),
        ],
        compiler_params=pltpu.CompilerParams(
            collective_id=0, has_side_effects=True, vmem_limit_bytes=48 << 20
        ),
    )(genotypes, observed, proportions, frequencies)


def solution(mesh):
    placed = (P("samp", "var"), P("samp", "var"), P(None, "samp"), P(None, ("samp", "var")))
    return jax.shard_map(
        local,
        mesh=mesh,
        in_specs=placed,
        out_specs=(P(None, "samp"), P(None, "var")),
        check_vma=False,
    )
```

```python
import jax
import jax.numpy as jnp
from jax import lax
from jax.experimental import pallas as pl
from jax.experimental.pallas import tpu as pltpu
from jax.sharding import PartitionSpec as P

STEPS = 2
CLIP_LOW = 1e-05
NORM_EPS = 1e-10
MESH = pl.DeviceIdType.MESH

K = 10
ROWS = 16
NS = 32
NV = 4
SAMP = 1024
VARS = 1024
LANES = 128
TILES = VARS // LANES
PIECES = 24
RB = 256
CB = 256
BLOCKS = VARS // CB
CHUNK = 128
CHUNKS = SAMP // CHUNK

F32 = jnp.float32
BF16 = jnp.bfloat16


def clip_unit(values):
    return jnp.clip(values, CLIP_LOW, 1.0 - CLIP_LOW)


def split3(values):
    high = values.astype(BF16).astype(F32)
    rest = values - high
    mid = rest.astype(BF16).astype(F32)
    low = (rest - mid).astype(BF16).astype(F32)
    return high, mid, low


def split2(values):
    high = values.astype(BF16)
    low = (values - high.astype(F32)).astype(BF16)
    return high, low


def dot(a, b):
    return lax.dot_general(
        a, b, (((1,), (0,)), ((), ())), preferred_element_type=F32
    )


def kernel(
    geno_hbm,
    seen_hbm,
    props_ref,
    freqs_ref,
    mix_ref,
    allele_ref,
    geno_buf,
    seen_buf,
    alt_cnt,
    ref_cnt,
    count_acc,
    prop_acc,
    q_now,
    q_start,
    q_one,
    p_now,
    p_start,
    p_one,
    q_cols,
    p_rows,
    q_rows,
    p_cols,
    w_buf,
    props_buf,
    freqs_buf,
    f_send,
    f_recv,
    rs_send,
    rs_recv,
    ag_all,
    z_all,
    sq_q,
    sq_p,
    load_sem,
    small_sem,
    f_sems,
    rs_sems,
    ag_sems,
    z_send,
    z_recv,
    sq_sems,
    sp_sems,
):
    s = lax.axis_index("samp")
    v = lax.axis_index("var")
    my_piece = lax.rem(s, 2) * 16 + s // 2
    is_owner = my_piece < PIECES
    my_q = my_piece // TILES
    my_t = lax.rem(my_piece, TILES)
    home = s // TILES

    def remote(src, dst, send_sem, recv_sem, where):
        return pltpu.make_async_remote_copy(
            src_ref=src,
            dst_ref=dst,
            send_sem=send_sem,
            recv_sem=recv_sem,
            device_id=where,
            device_id_type=MESH,
        )

    def wait_bytes(ref, sem):
        pltpu.make_async_copy(ref, ref, sem).wait()

    def load(chunk):
        rows = pl.ds(chunk * CHUNK, CHUNK)
        return (
            pltpu.make_async_copy(geno_hbm.at[rows], geno_buf.at[rows], load_sem.at[0, chunk]),
            pltpu.make_async_copy(seen_hbm.at[rows], seen_buf.at[rows], load_sem.at[1, chunk]),
        )

    small = (
        pltpu.make_async_copy(freqs_ref, freqs_buf, small_sem.at[0]),
        pltpu.make_async_copy(props_ref, props_buf, small_sem.at[1]),
    )
    for copy in small:
        copy.start()
    for chunk in range(CHUNKS):
        for copy in load(chunk):
            copy.start()

    barrier = pltpu.get_barrier_semaphore()

    def greet(where):
        pl.semaphore_signal(barrier, inc=1, device_id=where, device_id_type=MESH)

    def greet_samp(d, carry):
        greet((lax.rem(s + d, NS), v))
        return carry

    def greet_var(d, carry):
        greet((s, lax.rem(v + d, NV)))
        return carry

    def greet_source(i, carry):
        far_s = v * TILES + i // NV
        far_v = lax.rem(i, NV)

        @pl.when(jnp.logical_or(far_s != s, far_v != v))
        def _():
            greet((far_s, far_v))

        return carry

    lax.fori_loop(0, NS, greet_source, 0)
    lax.fori_loop(1, NV, greet_var, 0)
    lax.fori_loop(1, NS, greet_samp, 0)

    row_ids = lax.broadcasted_iota(jnp.int32, (ROWS, 1), 0)
    row_mask = row_ids < K

    small[0].wait()
    block = freqs_buf[...]
    tail = jnp.concatenate([block[8:K], jnp.zeros((ROWS - K, 32), F32)], axis=0)
    f_send[...] = jnp.concatenate([block[:8], tail, jnp.zeros((8, 64), F32)], axis=1)

    @pl.when(home == v)
    def _():
        pl.semaphore_wait(barrier, NS - 1 + NV - 1 + NS - 1)

    @pl.when(home != v)
    def _():
        pl.semaphore_wait(barrier, NS - 1 + NV - 1 + NS)

    my_slot = NV * lax.rem(s, TILES) + v

    def send_block(d, carry):
        far_s = lax.rem(s + NS // 2 + d, NS)

        @pl.when(jnp.logical_or(far_s != s, home != v))
        def _():
            remote(f_send, f_recv.at[my_slot], f_sems.at[0], f_sems.at[1], (far_s, home)).start()

        return carry

    lax.fori_loop(0, NS, send_block, 0)

    small[1].wait()
    q_now[...] = jnp.concatenate([props_buf[...], jnp.zeros((ROWS - K, SAMP), F32)], axis=0)

    def prep_q(q):
        qh, qm, ql = split3(q)
        pad = jnp.zeros((2 * ROWS, SAMP), F32)
        q_cols[...] = jnp.concatenate([qh, qh, qm, qm, qh, ql, pad], axis=0).T.astype(BF16)
        q_rows[...] = jnp.concatenate([qh, qm, ql], axis=0).astype(BF16)

    prep_q(q_now[...])

    lane_ids = lax.broadcasted_iota(jnp.int32, (VARS, LANES), 1)
    count_w = jnp.where(lane_ids == 3 * ROWS + K, 2.0, 0.0).astype(BF16)

    def convert(chunk):
        for copy in load(chunk):
            copy.wait()
        rows = pl.ds(chunk * CHUNK, CHUNK)
        seen = seen_buf[rows, :].astype(F32)
        alt = seen * geno_buf[rows, :].astype(F32)
        alt_cnt[rows, :] = alt
        ref_cnt[rows, :] = 2.0 * seen - alt
        count_acc[rows, :] = dot(seen.astype(BF16), count_w)

    for chunk in range(CHUNKS):
        convert(chunk)

    @pl.when(home == v)
    def _():
        wait_bytes(f_recv.at[pl.ds(0, NS - 1)], f_sems.at[1])
        f_recv[my_slot] = f_send[...]

    @pl.when(home != v)
    def _():
        wait_bytes(f_recv, f_sems.at[1])

    lane_group = lax.broadcasted_iota(jnp.int32, (8, LANES), 1) // 32
    for t in range(TILES):
        halves = []
        for half in range(2):
            rows8 = jnp.zeros((8, LANES), F32)
            for m in range(NV):
                shift = (32 * (m - half)) % LANES
                got = f_recv[NV * t + m]
                got = pltpu.roll(got, shift, 1) if shift else got
                rows8 = jnp.where(lane_group == m, got, rows8)
            halves.append(rows8)
        p_now[t] = jnp.concatenate(halves, axis=0)

    @pl.when(home == v)
    def _():
        wait_bytes(f_recv.at[pl.ds(0, NS - 1)], f_sems.at[0])

    @pl.when(home != v)
    def _():
        wait_bytes(f_recv, f_sems.at[0])

    def full_p(ref):
        return jnp.concatenate([ref[t] for t in range(TILES)], axis=1)

    def em_step(step, carry):
        phase = lax.rem(step, 3)
        parity = lax.rem(step, 2)
        p = full_p(p_now)
        ph, pm, pL = split3(p)
        pad = jnp.zeros((2 * ROWS, VARS), F32)
        pad5 = jnp.zeros((5 * ROWS, VARS), F32)
        p_rows[...] = jnp.concatenate([ph, pm, ph, pm, pL, ph, pad], axis=0).astype(BF16)
        turned_p = jnp.concatenate([ph, pm, pL, pad5], axis=0).T
        for cb in range(BLOCKS):
            pos = turned_p[cb * CB : (cb + 1) * CB].astype(BF16)
            neg = -pos
            for kind in range(4):
                p_cols[cb, kind * CB : (kind + 1) * CB, :] = pos if kind < 2 else neg

        def stage_a(cb, rb, slot):
            cols = pl.ds(cb * CB, CB)
            rows = pl.ds(rb * RB, RB)
            expected = dot(q_cols[rows, :], p_rows[:, cols])
            other = 1.0 - expected
            inverse = 1.0 / (expected * other)
            alt_high, alt_low = split2(alt_cnt[rows, cols] * (other * inverse))
            ref_high, ref_low = split2(ref_cnt[rows, cols] * (expected * inverse))
            for kind, part in enumerate((alt_high, alt_low, ref_high, ref_low)):
                w_buf[slot, :, kind * CB : (kind + 1) * CB] = part

        def stage_b(cb, rb, slot, sums):
            rows = pl.ds(rb * RB, RB)
            terms = w_buf[slot]
            part = dot(q_rows[:, rows], terms)
            sums = part if sums is None else sums + part
            before = count_acc[rows, :] if cb == 0 else prop_acc[rows, :]
            prop_acc[rows, :] = before + dot(terms, p_cols[cb])
            return sums

        def send_pieces(cb, sums):
            folded = sums[:ROWS] + sums[ROWS : 2 * ROWS] + sums[2 * ROWS :]
            alt = folded[:, :CB] + folded[:, CB : 2 * CB]
            ref = folded[:, 2 * CB : 3 * CB] + folded[:, 3 * CB :]
            for t in range(cb * CB // LANES, (cb + 1) * CB // LANES):
                lane = t * LANES - cb * CB
                for part in range(3):
                    piece = part * TILES + t
                    target = (piece % 16) * 2 + piece // 16
                    rs_send[piece] = jnp.concatenate(
                        [
                            alt[4 * part : 4 * part + 4, lane : lane + LANES],
                            ref[4 * part : 4 * part + 4, lane : lane + LANES],
                        ],
                        axis=0,
                    )

                    @pl.when(s != target)
                    def _():
                        remote(
                            rs_send.at[piece],
                            rs_recv.at[s],
                            rs_sems.at[0],
                            rs_sems.at[1],
                            (target, v),
                        ).start()

        units = [(cb, rb) for cb in range(BLOCKS) for rb in range(SAMP // RB)]
        sums = None
        stage_a(*units[0], 0)
        for n, (cb, rb) in enumerate(units):
            if n + 1 < len(units):
                stage_a(*units[n + 1], (n + 1) % 2)
            sums = stage_b(cb, rb, n % 2, sums)
            if rb == SAMP // RB - 1:
                send_pieces(cb, sums)
                sums = None

        turned = prop_acc[...].T
        z_all[parity, v] = (
            turned[:ROWS]
            + turned[ROWS : 2 * ROWS]
            + turned[2 * ROWS : 3 * ROWS]
            + turned[3 * ROWS : 4 * ROWS]
        )

        def send_z(d, carry):
            slot = z_all.at[parity, v]
            remote(slot, slot, z_send.at[0], z_recv.at[parity], (s, lax.rem(v + d, NV))).start()
            return carry

        lax.fori_loop(1, NV, send_z, 0)

        @pl.when(is_owner)
        def _():
            wait_bytes(rs_recv.at[pl.ds(0, NS - 1)], rs_sems.at[1])
            rs_recv[s] = rs_send[my_piece]
            sums = [rs_recv[i] for i in range(NS)]
            while len(sums) > 1:
                sums = [sums[i] + sums[i + 1] for i in range(0, len(sums), 2)]
            alt_sum, ref_sum = sums[0][:4], sums[0][4:]
            tile = p_now[my_t]
            old = jnp.where(my_q == 0, tile[:4], jnp.where(my_q == 1, tile[4:8], tile[8:12]))
            weighted = old * alt_sum
            new = clip_unit(weighted / (weighted + (1.0 - old) * ref_sum))
            piece_row = 4 * my_q + lax.broadcasted_iota(jnp.int32, (4, LANES), 0)
            ag_all[my_piece] = jnp.where(piece_row < K, new, 0.0)

            def send_ag(d, carry):
                slot = ag_all.at[my_piece]
                remote(slot, slot, ag_sems.at[0], ag_sems.at[1], (lax.rem(s + d, NS), v)).start()
                return carry

            lax.fori_loop(1, NS, send_ag, 0)

        wait_bytes(z_all.at[parity, pl.ds(0, NV - 1)], z_recv.at[parity])
        q = q_now[...]
        total = z_all[parity, 0] + z_all[parity, 1] + z_all[parity, 2] + z_all[parity, 3]
        twice = total[K : K + 1, :]
        inner = jnp.sum(q * total, axis=0, keepdims=True)
        q_next = jnp.where(row_mask, clip_unit(q * (1.0 + (total - inner) / twice)), 0.0)

        @pl.when(phase == 1)
        def _():
            step_mix = q_one[...] - q_start[...]
            curve_mix = q_next - q_one[...] - step_mix
            row = [jnp.sum(a * a, axis=0, keepdims=True) for a in (step_mix, curve_mix)]
            row = jnp.concatenate(row, axis=0)
            part = row[:, :LANES]
            for t in range(1, TILES):
                part = part + row[:, t * LANES : (t + 1) * LANES]
            sq_q[s] = part

            def send_sq(d, carry):
                slot = sq_q.at[s]
                remote(slot, slot, sq_sems.at[0], sq_sems.at[1], (lax.rem(s + d, NS), v)).start()
                return carry

            lax.fori_loop(1, NS, send_sq, 0)

        @pl.when(phase != 1)
        def _():
            prep_q(q_next)

        @pl.when(is_owner)
        def _():
            wait_bytes(ag_all.at[pl.ds(0, PIECES - 1)], ag_sems.at[1])

        @pl.when(jnp.logical_not(is_owner))
        def _():
            wait_bytes(ag_all, ag_sems.at[1])

        zeros4 = jnp.zeros((4, LANES), F32)
        p_next = [
            jnp.concatenate([ag_all[t], ag_all[TILES + t], ag_all[2 * TILES + t], zeros4], axis=0)
            for t in range(TILES)
        ]

        @pl.when(phase == 0)
        def _():
            q_start[...] = q
            q_one[...] = q_next
            q_now[...] = q_next
            for t in range(TILES):
                p_start[t] = p_now[t]
                p_one[t] = p_next[t]
                p_now[t] = p_next[t]

        @pl.when(phase == 2)
        def _():
            q_now[...] = q_next
            for t in range(TILES):
                p_now[t] = p_next[t]

        @pl.when(phase == 1)
        def _():
            part_r = jnp.zeros((ROWS, LANES), F32)
            part_v = jnp.zeros((ROWS, LANES), F32)
            for t in range(TILES):
                r = p_one[t] - p_start[t]
                c = p_next[t] - p_one[t] - r
                part_r = part_r + r * r
                part_v = part_v + c * c
            sq_p[v] = jnp.concatenate(
                [jnp.sum(part_r, axis=0, keepdims=True), jnp.sum(part_v, axis=0, keepdims=True)],
                axis=0,
            )

            def send_sp(d, carry):
                slot = sq_p.at[v]
                remote(slot, slot, sp_sems.at[0], sp_sems.at[1], (s, lax.rem(v + d, NV))).start()
                return carry

            lax.fori_loop(1, NV, send_sp, 0)

            def alpha_of(sums):
                first = jnp.sum(sums[0:1], axis=1, keepdims=True)
                second = jnp.sum(sums[1:2], axis=1, keepdims=True)
                return jnp.maximum(1.0, jnp.sqrt(first / (second + NORM_EPS)))

            wait_bytes(sq_q.at[pl.ds(0, NS - 1)], sq_sems.at[1])
            sums = [sq_q[i] for i in range(NS)]
            while len(sums) > 1:
                sums = [sums[i] + sums[i + 1] for i in range(0, len(sums), 2)]
            alpha = alpha_of(sums[0])
            base = q_start[...]
            step_mix = q_one[...] - base
            curve_mix = q_next - q_one[...] - step_mix
            extra = clip_unit(base + 2.0 * alpha * step_mix + alpha * alpha * curve_mix)
            extra = jnp.where(row_mask, extra, 0.0)
            extra = extra / jnp.sum(extra, axis=0, keepdims=True)
            q_now[...] = extra
            prep_q(extra)

            wait_bytes(sq_p.at[pl.ds(0, NV - 1)], sp_sems.at[1])
            alpha_p = alpha_of(sq_p[0] + sq_p[1] + sq_p[2] + sq_p[3])
            for t in range(TILES):
                base_p = p_start[t]
                r = p_one[t] - base_p
                c = p_next[t] - p_one[t] - r
                extra_p = clip_unit(base_p + 2.0 * alpha_p * r + alpha_p * alpha_p * c)
                p_now[t] = jnp.where(row_mask, extra_p, 0.0)

            wait_bytes(sq_q.at[pl.ds(0, NS - 1)], sq_sems.at[0])
            wait_bytes(sq_p.at[pl.ds(0, NV - 1)], sp_sems.at[0])

        wait_bytes(z_all.at[parity, pl.ds(0, NV - 1)], z_send.at[0])
        wait_bytes(rs_send.at[pl.ds(0, PIECES - 1)], rs_sems.at[0])

        @pl.when(is_owner)
        def _():
            wait_bytes(ag_all, ag_sems.at[0])
            wait_bytes(ag_all.at[pl.ds(0, NS - 1 - PIECES)], ag_sems.at[0])

        @pl.when(jnp.logical_not(is_owner))
        def _():
            wait_bytes(rs_send.at[0], rs_sems.at[0])

        return carry

    lax.fori_loop(0, 3 * STEPS, em_step, 0)
    mix_ref[...] = q_now[:K, :]
    for t in range(TILES):
        allele_ref[:, t * LANES : (t + 1) * LANES] = p_now[t][:K]


def local(genotypes, observed, proportions, frequencies):
    vmem = pl.BlockSpec(memory_space=pltpu.VMEM)
    hbm = pl.BlockSpec(memory_space=pl.ANY)
    dma = pltpu.SemaphoreType.DMA
    return pl.pallas_call(
        kernel,
        name="em",
        out_shape=(
            jax.ShapeDtypeStruct((K, SAMP), F32),
            jax.ShapeDtypeStruct((K, VARS), F32),
        ),
        in_specs=[hbm, hbm, hbm, hbm],
        out_specs=(vmem, vmem),
        scratch_shapes=[
            pltpu.VMEM((SAMP, VARS), jnp.int32),
            pltpu.VMEM((SAMP, VARS), jnp.int32),
            pltpu.VMEM((SAMP, VARS), F32),
            pltpu.VMEM((SAMP, VARS), F32),
            pltpu.VMEM((SAMP, LANES), F32),
            pltpu.VMEM((SAMP, LANES), F32),
            pltpu.VMEM((ROWS, SAMP), F32),
            pltpu.VMEM((ROWS, SAMP), F32),
            pltpu.VMEM((ROWS, SAMP), F32),
            pltpu.VMEM((TILES, ROWS, LANES), F32),
            pltpu.VMEM((TILES, ROWS, LANES), F32),
            pltpu.VMEM((TILES, ROWS, LANES), F32),
            pltpu.VMEM((SAMP, LANES), BF16),
            pltpu.VMEM((LANES, VARS), BF16),
            pltpu.VMEM((3 * ROWS, SAMP), BF16),
            pltpu.VMEM((BLOCKS, 4 * CB, LANES), BF16),
            pltpu.VMEM((2, RB, 4 * CB), BF16),
            pltpu.VMEM((K, SAMP), F32),
            pltpu.VMEM((K, 32), F32),
            pltpu.VMEM((8, LANES), F32),
            pltpu.VMEM((NS, 8, LANES), F32),
            pltpu.VMEM((PIECES, 8, LANES), F32),
            pltpu.VMEM((NS, 8, LANES), F32),
            pltpu.VMEM((PIECES, 4, LANES), F32),
            pltpu.VMEM((2, NV, ROWS, SAMP), F32),
            pltpu.VMEM((NS, 2, LANES), F32),
            pltpu.VMEM((NV, 2, LANES), F32),
            dma((2, CHUNKS)),
            dma((2,)),
            dma((2,)),
            dma((2,)),
            dma((2,)),
            dma((1,)),
            dma((2,)),
            dma((2,)),
            dma((2,)),
        ],
        compiler_params=pltpu.CompilerParams(
            collective_id=0, has_side_effects=True, vmem_limit_bytes=60 * 1024 * 1024
        ),
    )(genotypes, observed, proportions, frequencies)


def solution(mesh):
    placed = (P("samp", "var"), P("samp", "var"), P(None, "samp"), P(None, ("samp", "var")))
    return jax.shard_map(
        local,
        mesh=mesh,
        in_specs=placed,
        out_specs=(P(None, "samp"), P(None, "var")),
        check_vma=False,
    )
```

```python
import jax
import jax.numpy as jnp
from jax import lax
from jax.experimental import pallas as pl
from jax.experimental.pallas import tpu as pltpu
from jax.sharding import PartitionSpec as P

STEPS = 2
CLIP_LOW = 1e-05
NORM_EPS = 1e-10
MESH = pl.DeviceIdType.MESH

K = 10
ROWS = 16
NS = 32
NV = 4
SAMP = 1024
VARS = 1024
LANES = 128
TILES = VARS // LANES
PIECES = 24
RB = 256
CB = 256
BLOCKS = VARS // CB
GROUP = CB // LANES
CHUNK = 128
CHUNKS = SAMP // CHUNK

F32 = jnp.float32
BF16 = jnp.bfloat16


def clip_unit(values):
    return jnp.clip(values, CLIP_LOW, 1.0 - CLIP_LOW)


def split3(values):
    high = values.astype(BF16).astype(F32)
    rest = values - high
    mid = rest.astype(BF16).astype(F32)
    low = (rest - mid).astype(BF16).astype(F32)
    return high, mid, low


def split2(values):
    high = values.astype(BF16)
    low = (values - high.astype(F32)).astype(BF16)
    return high, low


def dot(a, b):
    return lax.dot_general(
        a, b, (((1,), (0,)), ((), ())), preferred_element_type=F32
    )


def dot_t(a, b):
    return lax.dot_general(
        a, b, (((1,), (1,)), ((), ())), preferred_element_type=F32
    )


def kernel(
    geno_hbm,
    seen_hbm,
    props_ref,
    freqs_ref,
    mix_ref,
    allele_ref,
    geno_buf,
    seen_buf,
    alt_cnt,
    ref_cnt,
    count_acc,
    prop_acc,
    q_now,
    q_start,
    p_now,
    p_start,
    q_cols,
    p_rows,
    q_rows,
    p_three,
    w_buf,
    props_buf,
    freqs_buf,
    f_send,
    f_recv,
    rs_send,
    rs_recv,
    ag_all,
    z_all,
    sq_q,
    sq_p,
    load_sem,
    small_sem,
    f_sems,
    rs_sems,
    ag_send,
    ag_recv,
    z_send,
    z_recv,
    sq_sems,
    sp_sems,
):
    s = lax.axis_index("samp")
    v = lax.axis_index("var")
    my_piece = lax.rem(s, 2) * 16 + s // 2
    is_owner = my_piece < PIECES
    my_q = my_piece // TILES
    my_t = lax.rem(my_piece, TILES)
    home = s // TILES

    def remote(src, dst, send_sem, recv_sem, where):
        return pltpu.make_async_remote_copy(
            src_ref=src,
            dst_ref=dst,
            send_sem=send_sem,
            recv_sem=recv_sem,
            device_id=where,
            device_id_type=MESH,
        )

    def wait_bytes(ref, sem):
        pltpu.make_async_copy(ref, ref, sem).wait()

    def load(chunk):
        rows = pl.ds(chunk * CHUNK, CHUNK)
        return (
            pltpu.make_async_copy(geno_hbm.at[rows], geno_buf.at[rows], load_sem.at[0, chunk]),
            pltpu.make_async_copy(seen_hbm.at[rows], seen_buf.at[rows], load_sem.at[1, chunk]),
        )

    small = (
        pltpu.make_async_copy(freqs_ref, freqs_buf, small_sem.at[0]),
        pltpu.make_async_copy(props_ref, props_buf, small_sem.at[1]),
    )
    for copy in small:
        copy.start()
    for chunk in range(CHUNKS):
        for copy in load(chunk):
            copy.start()

    barrier = pltpu.get_barrier_semaphore()

    def greet(where):
        pl.semaphore_signal(barrier, inc=1, device_id=where, device_id_type=MESH)

    def greet_samp(d, carry):
        greet((lax.rem(s + d, NS), v))
        return carry

    def greet_var(d, carry):
        greet((s, lax.rem(v + d, NV)))
        return carry

    def greet_source(i, carry):
        far_s = v * TILES + i // NV
        far_v = lax.rem(i, NV)

        @pl.when(jnp.logical_or(far_s != s, far_v != v))
        def _():
            greet((far_s, far_v))

        return carry

    lax.fori_loop(0, NS, greet_source, 0)
    lax.fori_loop(1, NV, greet_var, 0)
    lax.fori_loop(1, NS, greet_samp, 0)

    row_ids = lax.broadcasted_iota(jnp.int32, (ROWS, 1), 0)
    row_mask = row_ids < K

    small[0].wait()
    block = freqs_buf[...]
    tail = jnp.concatenate([block[8:K], jnp.zeros((ROWS - K, 32), F32)], axis=0)
    f_send[...] = jnp.concatenate([block[:8], tail, jnp.zeros((8, 64), F32)], axis=1)

    @pl.when(home == v)
    def _():
        pl.semaphore_wait(barrier, NS - 1 + NV - 1 + NS - 1)

    @pl.when(home != v)
    def _():
        pl.semaphore_wait(barrier, NS - 1 + NV - 1 + NS)

    my_slot = NV * lax.rem(s, TILES) + v

    def send_block(d, carry):
        far_s = lax.rem(s + NS // 2 + d, NS)

        @pl.when(jnp.logical_or(far_s != s, home != v))
        def _():
            remote(f_send, f_recv.at[my_slot], f_sems.at[0], f_sems.at[1], (far_s, home)).start()

        return carry

    lax.fori_loop(0, NS, send_block, 0)

    small[1].wait()
    q_now[...] = jnp.concatenate([props_buf[...], jnp.zeros((ROWS - K, SAMP), F32)], axis=0)

    def prep_q(q):
        qh, qm, ql = split3(q)
        pad = jnp.zeros((2 * ROWS, SAMP), F32)
        q_cols[...] = jnp.concatenate([qh, qh, qm, qm, qh, ql, pad], axis=0).T.astype(BF16)
        q_rows[...] = jnp.concatenate([qh, qm, ql], axis=0).astype(BF16)

    prep_q(q_now[...])

    count_rows = lax.broadcasted_iota(jnp.int32, (ROWS, VARS), 0)
    count_w = jnp.where(count_rows == K, 2.0, 0.0).astype(BF16)

    def convert(chunk):
        for copy in load(chunk):
            copy.wait()
        rows = pl.ds(chunk * CHUNK, CHUNK)
        seen = seen_buf[rows, :].astype(F32)
        alt = seen * geno_buf[rows, :].astype(F32)
        alt_cnt[rows, :] = alt
        ref_cnt[rows, :] = 2.0 * seen - alt
        count_acc[:, rows] = dot_t(count_w, seen.astype(BF16))

    for chunk in range(CHUNKS):
        convert(chunk)

    @pl.when(home == v)
    def _():
        wait_bytes(f_recv.at[pl.ds(0, NS - 1)], f_sems.at[1])
        f_recv[my_slot] = f_send[...]

    @pl.when(home != v)
    def _():
        wait_bytes(f_recv, f_sems.at[1])

    lane_group = lax.broadcasted_iota(jnp.int32, (8, LANES), 1) // 32
    for t in range(TILES):
        halves = []
        for half in range(2):
            rows8 = jnp.zeros((8, LANES), F32)
            for m in range(NV):
                shift = (32 * (m - half)) % LANES
                got = f_recv[NV * t + m]
                got = pltpu.roll(got, shift, 1) if shift else got
                rows8 = jnp.where(lane_group == m, got, rows8)
            halves.append(rows8)
        p_now[t] = jnp.concatenate(halves, axis=0)

    @pl.when(home == v)
    def _():
        wait_bytes(f_recv.at[pl.ds(0, NS - 1)], f_sems.at[0])

    @pl.when(home != v)
    def _():
        wait_bytes(f_recv, f_sems.at[0])

    def wait_alleles(cb):
        mine = jnp.logical_and(is_owner, my_t // GROUP == cb)

        @pl.when(mine)
        def _():
            wait_bytes(ag_all.at[pl.ds(0, 3 * GROUP - 1)], ag_recv.at[cb])

        @pl.when(jnp.logical_not(mine))
        def _():
            wait_bytes(ag_all.at[pl.ds(0, 3 * GROUP)], ag_recv.at[cb])

    def wait_alleles_sent():
        @pl.when(is_owner)
        def _():
            wait_bytes(ag_all, ag_send.at[0])
            wait_bytes(ag_all.at[pl.ds(0, NS - 1 - PIECES)], ag_send.at[0])

    def tile_of(t):
        return jnp.concatenate(
            [ag_all[t], ag_all[TILES + t], ag_all[2 * TILES + t], jnp.zeros((4, LANES), F32)],
            axis=0,
        )

    def em_step(step, carry):
        phase = lax.rem(step, 3)
        parity = lax.rem(step, 2)
        follows = jnp.logical_or(phase == 1, jnp.logical_and(phase == 0, step > 0))

        def prep_p(cb):
            @pl.when(follows)
            def _():
                wait_alleles(cb)
                for t in range(cb * GROUP, (cb + 1) * GROUP):
                    p_start[t] = p_now[t]
                    p_now[t] = tile_of(t)

            p = jnp.concatenate([p_now[t] for t in range(cb * GROUP, (cb + 1) * GROUP)], axis=1)
            ph, pm, pL = split3(p)
            pad = jnp.zeros((2 * ROWS, CB), F32)
            cols = pl.ds(cb * CB, CB)
            p_rows[:, cols] = jnp.concatenate([ph, pm, ph, pm, pL, ph, pad], axis=0).astype(BF16)
            p_three[...] = jnp.concatenate([ph, pm, pL], axis=0).astype(BF16)

        def stage_a(cb, rb, slot):
            cols = pl.ds(cb * CB, CB)
            rows = pl.ds(rb * RB, RB)
            expected = dot(q_cols[rows, :], p_rows[:, cols])
            other = 1.0 - expected
            inverse = 1.0 / (expected * other)
            alt_high, alt_low = split2(alt_cnt[rows, cols] * (other * inverse))
            ref_high, ref_low = split2(ref_cnt[rows, cols] * (expected * inverse))
            for kind, part in enumerate((alt_high, alt_low, ref_high, ref_low)):
                w_buf[slot, kind] = part

        def stage_b(cb, rb, slot, sums):
            rows = pl.ds(rb * RB, RB)
            q_part = q_rows[:, rows]
            p_part = p_three[...]
            sides = []
            props = []
            for side in range(2):
                high, low = w_buf[slot, 2 * side], w_buf[slot, 2 * side + 1]
                sides.append(dot(q_part, high) + dot(q_part, low))
                props.append(dot_t(p_part, high) + dot_t(p_part, low))
            prop = props[0] - props[1]
            prop_acc[:, rows] = prop if cb == 0 else prop_acc[:, rows] + prop
            return sides if sums is None else [sums[i] + sides[i] for i in range(2)]

        def send_pieces(cb, sums):
            alt, ref = [a[:ROWS] + a[ROWS : 2 * ROWS] + a[2 * ROWS :] for a in sums]
            for t in range(cb * CB // LANES, (cb + 1) * CB // LANES):
                lane = t * LANES - cb * CB
                for part in range(3):
                    piece = part * TILES + t
                    target = (piece % 16) * 2 + piece // 16
                    rs_send[piece] = jnp.concatenate(
                        [
                            alt[4 * part : 4 * part + 4, lane : lane + LANES],
                            ref[4 * part : 4 * part + 4, lane : lane + LANES],
                        ],
                        axis=0,
                    )

                    @pl.when(s != target)
                    def _():
                        remote(
                            rs_send.at[piece],
                            rs_recv.at[s],
                            rs_sems.at[0],
                            rs_sems.at[1],
                            (target, v),
                        ).start()

        for cb in range(BLOCKS):
            prep_p(cb)
            sums = None
            stage_a(cb, 0, 0)
            for rb in range(SAMP // RB):
                if rb + 1 < SAMP // RB:
                    stage_a(cb, rb + 1, (rb + 1) % 2)
                sums = stage_b(cb, rb, rb % 2, sums)
            send_pieces(cb, sums)

        z_all[parity, v] = count_acc[...] + (
            prop_acc[:ROWS, :] + prop_acc[ROWS : 2 * ROWS, :] + prop_acc[2 * ROWS :, :]
        )

        def send_z(d, carry):
            slot = z_all.at[parity, v]
            remote(slot, slot, z_send.at[0], z_recv.at[parity], (s, lax.rem(v + d, NV))).start()
            return carry

        lax.fori_loop(1, NV, send_z, 0)

        @pl.when(is_owner)
        def _():
            wait_bytes(rs_recv.at[pl.ds(0, NS - 1)], rs_sems.at[1])
            rs_recv[s] = rs_send[my_piece]
            sums = [rs_recv[i] for i in range(NS)]
            while len(sums) > 1:
                sums = [sums[i] + sums[i + 1] for i in range(0, len(sums), 2)]
            alt_sum, ref_sum = sums[0][:4], sums[0][4:]
            tile = p_now[my_t]
            old = jnp.where(my_q == 0, tile[:4], jnp.where(my_q == 1, tile[4:8], tile[8:12]))
            weighted = old * alt_sum
            new = clip_unit(weighted / (weighted + (1.0 - old) * ref_sum))
            piece_row = 4 * my_q + lax.broadcasted_iota(jnp.int32, (4, LANES), 0)

            @pl.when(step > 0)
            def _():
                wait_alleles_sent()

            ag_all[my_piece] = jnp.where(piece_row < K, new, 0.0)

            def send_ag(d, carry):
                slot = ag_all.at[my_piece]
                remote(
                    slot, slot, ag_send.at[0], ag_recv.at[my_t // GROUP], (lax.rem(s + d, NS), v)
                ).start()
                return carry

            lax.fori_loop(1, NS, send_ag, 0)

        wait_bytes(z_all.at[parity, pl.ds(0, NV - 1)], z_recv.at[parity])
        q = q_now[...]
        total = z_all[parity, 0] + z_all[parity, 1] + z_all[parity, 2] + z_all[parity, 3]
        twice = total[K : K + 1, :]
        inner = jnp.sum(q * total, axis=0, keepdims=True)
        q_next = jnp.where(row_mask, clip_unit(q * (1.0 + (total - inner) / twice)), 0.0)

        @pl.when(phase == 1)
        def _():
            step_mix = q - q_start[...]
            curve_mix = q_next - q - step_mix
            row = [jnp.sum(a * a, axis=0, keepdims=True) for a in (step_mix, curve_mix)]
            row = jnp.concatenate(row, axis=0)
            part = row[:, :LANES]
            for t in range(1, TILES):
                part = part + row[:, t * LANES : (t + 1) * LANES]
            sq_q[s] = part

            def send_sq(d, carry):
                slot = sq_q.at[s]
                remote(slot, slot, sq_sems.at[0], sq_sems.at[1], (lax.rem(s + d, NS), v)).start()
                return carry

            lax.fori_loop(1, NS, send_sq, 0)

        @pl.when(phase != 1)
        def _():
            q_start[...] = q
            q_now[...] = q_next
            prep_q(q_next)

        @pl.when(phase == 1)
        def _():
            for cb in range(BLOCKS):
                wait_alleles(cb)
            p_next = [tile_of(t) for t in range(TILES)]
            part_r = jnp.zeros((ROWS, LANES), F32)
            part_v = jnp.zeros((ROWS, LANES), F32)
            for t in range(TILES):
                r = p_now[t] - p_start[t]
                c = p_next[t] - p_now[t] - r
                part_r = part_r + r * r
                part_v = part_v + c * c
            sq_p[v] = jnp.concatenate(
                [jnp.sum(part_r, axis=0, keepdims=True), jnp.sum(part_v, axis=0, keepdims=True)],
                axis=0,
            )

            def send_sp(d, carry):
                slot = sq_p.at[v]
                remote(slot, slot, sp_sems.at[0], sp_sems.at[1], (s, lax.rem(v + d, NV))).start()
                return carry

            lax.fori_loop(1, NV, send_sp, 0)

            def alpha_of(sums):
                first = jnp.sum(sums[0:1], axis=1, keepdims=True)
                second = jnp.sum(sums[1:2], axis=1, keepdims=True)
                return jnp.maximum(1.0, jnp.sqrt(first / (second + NORM_EPS)))

            wait_bytes(sq_q.at[pl.ds(0, NS - 1)], sq_sems.at[1])
            sums = [sq_q[i] for i in range(NS)]
            while len(sums) > 1:
                sums = [sums[i] + sums[i + 1] for i in range(0, len(sums), 2)]
            alpha = alpha_of(sums[0])
            base = q_start[...]
            step_mix = q - base
            curve_mix = q_next - q - step_mix
            extra = clip_unit(base + 2.0 * alpha * step_mix + alpha * alpha * curve_mix)
            extra = jnp.where(row_mask, extra, 0.0)
            extra = extra / jnp.sum(extra, axis=0, keepdims=True)
            q_now[...] = extra
            prep_q(extra)

            wait_bytes(sq_p.at[pl.ds(0, NV - 1)], sp_sems.at[1])
            alpha_p = alpha_of(sq_p[0] + sq_p[1] + sq_p[2] + sq_p[3])
            for t in range(TILES):
                base_p = p_start[t]
                r = p_now[t] - base_p
                c = p_next[t] - p_now[t] - r
                extra_p = clip_unit(base_p + 2.0 * alpha_p * r + alpha_p * alpha_p * c)
                p_now[t] = jnp.where(row_mask, extra_p, 0.0)

            wait_bytes(sq_q.at[pl.ds(0, NS - 1)], sq_sems.at[0])
            wait_bytes(sq_p.at[pl.ds(0, NV - 1)], sp_sems.at[0])

        wait_bytes(z_all.at[parity, pl.ds(0, NV - 1)], z_send.at[0])
        wait_bytes(rs_send.at[pl.ds(0, PIECES - 1)], rs_sems.at[0])

        @pl.when(jnp.logical_not(is_owner))
        def _():
            wait_bytes(rs_send.at[0], rs_sems.at[0])

        return carry

    lax.fori_loop(0, 3 * STEPS, em_step, 0)
    mix_ref[...] = q_now[:K, :]
    for cb in range(BLOCKS):
        wait_alleles(cb)
    for t in range(TILES):
        allele_ref[:, t * LANES : (t + 1) * LANES] = tile_of(t)[:K]
    wait_alleles_sent()


def finish(mix_in, allele_in, mix_out, allele_out):
    mix_out[...] = mix_in[...]
    allele_out[...] = allele_in[...]


def local(genotypes, observed, proportions, frequencies):
    vmem = pl.BlockSpec(memory_space=pltpu.VMEM)
    hbm = pl.BlockSpec(memory_space=pl.ANY)
    dma = pltpu.SemaphoreType.DMA
    outs = pl.pallas_call(
        kernel,
        name="em",
        out_shape=(
            jax.ShapeDtypeStruct((K, SAMP), F32),
            jax.ShapeDtypeStruct((K, VARS), F32),
        ),
        in_specs=[hbm, hbm, hbm, hbm],
        out_specs=(vmem, vmem),
        scratch_shapes=[
            pltpu.VMEM((SAMP, VARS), jnp.int32),
            pltpu.VMEM((SAMP, VARS), jnp.int32),
            pltpu.VMEM((SAMP, VARS), F32),
            pltpu.VMEM((SAMP, VARS), F32),
            pltpu.VMEM((ROWS, SAMP), F32),
            pltpu.VMEM((3 * ROWS, SAMP), F32),
            pltpu.VMEM((ROWS, SAMP), F32),
            pltpu.VMEM((ROWS, SAMP), F32),
            pltpu.VMEM((TILES, ROWS, LANES), F32),
            pltpu.VMEM((TILES, ROWS, LANES), F32),
            pltpu.VMEM((SAMP, LANES), BF16),
            pltpu.VMEM((LANES, VARS), BF16),
            pltpu.VMEM((3 * ROWS, SAMP), BF16),
            pltpu.VMEM((3 * ROWS, CB), BF16),
            pltpu.VMEM((2, 4, RB, CB), BF16),
            pltpu.VMEM((K, SAMP), F32),
            pltpu.VMEM((K, 32), F32),
            pltpu.VMEM((8, LANES), F32),
            pltpu.VMEM((NS, 8, LANES), F32),
            pltpu.VMEM((PIECES, 8, LANES), F32),
            pltpu.VMEM((NS, 8, LANES), F32),
            pltpu.VMEM((PIECES, 4, LANES), F32),
            pltpu.VMEM((2, NV, ROWS, SAMP), F32),
            pltpu.VMEM((NS, 2, LANES), F32),
            pltpu.VMEM((NV, 2, LANES), F32),
            dma((2, CHUNKS)),
            dma((2,)),
            dma((2,)),
            dma((2,)),
            dma((1,)),
            dma((BLOCKS,)),
            dma((1,)),
            dma((2,)),
            dma((2,)),
            dma((2,)),
        ],
        compiler_params=pltpu.CompilerParams(
            collective_id=0, has_side_effects=True, vmem_limit_bytes=60 * 1024 * 1024
        ),
    )(genotypes, observed, proportions, frequencies)
    return pl.pallas_call(
        finish,
        name="finish",
        out_shape=(
            jax.ShapeDtypeStruct((K, SAMP), F32),
            jax.ShapeDtypeStruct((K, VARS), F32),
        ),
        in_specs=[vmem, vmem],
        out_specs=(vmem, vmem),
    )(*outs)


def solution(mesh):
    placed = (P("samp", "var"), P("samp", "var"), P(None, "samp"), P(None, ("samp", "var")))
    return jax.shard_map(
        local,
        mesh=mesh,
        in_specs=placed,
        out_specs=(P(None, "samp"), P(None, "var")),
        check_vma=False,
    )
```

```python
import jax
import jax.numpy as jnp
from jax import lax
from jax.experimental import pallas as pl
from jax.experimental.pallas import tpu as pltpu
from jax.sharding import PartitionSpec as P

STEPS = 2
CLIP_LOW = 1e-05
NORM_EPS = 1e-10
MESH = pl.DeviceIdType.MESH

K = 10
ROWS = 16
NS = 32
NV = 4
SAMP = 1024
VARS = 1024
LANES = 128
TILES = VARS // LANES
HALF = K // 2
PIECES = 2 * TILES
SERVED = ((2, 0), (1, 1), (1, 3), (3, 0), (1, 0), (0, 3), (0, 1), (0, 0))
SPREAD = sorted(
    ((x, y, c) for x in range(4) for y in range(4) for c in range(2)),
    key=lambda d: -(min(d[0], 4 - d[0]) + min(d[1], 4 - d[1])),
)
RB = 256
CB = 256
BLOCKS = VARS // CB
GROUP = CB // LANES
CHUNK = 128
CHUNKS = SAMP // CHUNK

F32 = jnp.float32
BF16 = jnp.bfloat16


def clip_unit(values):
    return jnp.clip(values, CLIP_LOW, 1.0 - CLIP_LOW)


def split3(values):
    high = values.astype(BF16).astype(F32)
    rest = values - high
    mid = rest.astype(BF16).astype(F32)
    low = (rest - mid).astype(BF16).astype(F32)
    return high, mid, low


def dot(a, b):
    return lax.dot_general(
        a, b, (((1,), (0,)), ((), ())), preferred_element_type=F32
    )


def dot_t(a, b):
    return lax.dot_general(
        a, b, (((1,), (1,)), ((), ())), preferred_element_type=F32
    )


def kernel(
    geno_hbm,
    seen_hbm,
    props_ref,
    freqs_ref,
    mix_ref,
    allele_ref,
    geno_buf,
    seen_buf,
    alt_cnt,
    ref_cnt,
    count_acc,
    prop_acc,
    q_now,
    q_start,
    p_now,
    p_start,
    q_cols,
    p_rows,
    q_rows,
    p_three,
    w_buf,
    props_buf,
    freqs_buf,
    f_send,
    f_recv,
    rs_send,
    rs_recv,
    ag_all,
    z_top,
    z_rest,
    c_all,
    twice_ref,
    sq_q,
    sp_all,
    sp_out,
    load_sem,
    small_sem,
    f_sems,
    rs_sems,
    ag_send,
    ag_recv,
    z_send,
    z_recv,
    y_recv,
    c_sems,
    sq_sems,
    sp_sems,
):
    s = lax.axis_index("samp")
    v = lax.axis_index("var")
    chip_x = s // 8
    chip_y = lax.rem(s // 2, 4)
    core = lax.rem(s, 2)
    my_t = lax.rem(chip_x, 2) * 4 + lax.rem(chip_y + 2 * (chip_x // 2), 4)
    my_piece = core * TILES + my_t

    along_x = [lax.rem(chip_x + d, 4) * 8 for d in range(4)]
    along_y = [lax.rem(chip_y + d, 4) * 2 for d in range(4)]
    cores = (core, 1 - core)
    along_v = [lax.rem(v + d, NV) for d in range(NV)]

    def moved(x, y, c):
        return along_x[x] + along_y[y] + cores[c]

    home = s // TILES

    def remote(src, dst, send_sem, recv_sem, where):
        return pltpu.make_async_remote_copy(
            src_ref=src,
            dst_ref=dst,
            send_sem=send_sem,
            recv_sem=recv_sem,
            device_id=where,
            device_id_type=MESH,
        )

    def wait_bytes(ref, sem):
        pltpu.make_async_copy(ref, ref, sem).wait()

    def load(chunk):
        rows = pl.ds(chunk * CHUNK, CHUNK)
        return (
            pltpu.make_async_copy(geno_hbm.at[rows], geno_buf.at[rows], load_sem.at[0, chunk]),
            pltpu.make_async_copy(seen_hbm.at[rows], seen_buf.at[rows], load_sem.at[1, chunk]),
        )

    small = (
        pltpu.make_async_copy(freqs_ref, freqs_buf, small_sem.at[0]),
        pltpu.make_async_copy(props_ref, props_buf, small_sem.at[1]),
    )
    for copy in small:
        copy.start()
    for chunk in range(CHUNKS):
        for copy in load(chunk):
            copy.start()

    barrier = pltpu.get_barrier_semaphore()

    def greet(where):
        pl.semaphore_signal(barrier, inc=1, device_id=where, device_id_type=MESH)

    def greet_samp(d, carry):
        greet((lax.rem(s + d, NS), v))
        return carry

    def greet_var(d, carry):
        greet((s, lax.rem(v + d, NV)))
        return carry

    def greet_source(i, carry):
        far_s = v * TILES + i // NV
        far_v = lax.rem(i, NV)

        @pl.when(jnp.logical_or(far_s != s, far_v != v))
        def _():
            greet((far_s, far_v))

        return carry

    lax.fori_loop(0, NS, greet_source, 0)
    lax.fori_loop(1, NV, greet_var, 0)
    lax.fori_loop(1, NS, greet_samp, 0)

    row_ids = lax.broadcasted_iota(jnp.int32, (ROWS, 1), 0)
    row_mask = row_ids < K

    small[0].wait()
    block = freqs_buf[...]
    tail = jnp.concatenate([block[8:K], jnp.zeros((ROWS - K, 32), F32)], axis=0)
    f_send[...] = jnp.concatenate([block[:8], tail, jnp.zeros((8, 64), F32)], axis=1)

    @pl.when(home == v)
    def _():
        pl.semaphore_wait(barrier, NS - 1 + NV - 1 + NS - 1)

    @pl.when(home != v)
    def _():
        pl.semaphore_wait(barrier, NS - 1 + NV - 1 + NS)

    my_slot = NV * lax.rem(s, TILES) + v

    for x, y, c in SPREAD:
        copy = remote(f_send, f_recv.at[my_slot], f_sems.at[0], f_sems.at[1], (moved(x, y, c), home))
        if (x, y, c) != (0, 0, 0):
            copy.start()
        else:
            pl.when(home != v)(copy.start)

    small[1].wait()
    q_now[...] = jnp.concatenate([props_buf[...], jnp.zeros((ROWS - K, SAMP), F32)], axis=0)

    def prep_q(q):
        qh, qm, ql = split3(q)
        pad = jnp.zeros((2 * ROWS, SAMP), F32)
        q_cols[...] = jnp.concatenate([qh, qh, qm, qm, qh, ql, pad], axis=0).T.astype(BF16)
        q_rows[...] = jnp.concatenate([qh, qm, ql], axis=0).astype(BF16)

    prep_q(q_now[...])

    count_w = jnp.full((ROWS, VARS), 2.0, BF16)

    def convert(chunk):
        for copy in load(chunk):
            copy.wait()
        rows = pl.ds(chunk * CHUNK, CHUNK)
        seen = seen_buf[rows, :].astype(F32)
        alt = seen * geno_buf[rows, :].astype(F32)
        alt_cnt[rows, :] = alt
        ref_cnt[rows, :] = 2.0 * seen - alt
        count_acc[:, rows] = dot_t(count_w, seen.astype(BF16))

    for chunk in range(CHUNKS):
        convert(chunk)

    c_all[v] = count_acc[:1, :]
    c_slot = c_all.at[v]
    for d in (2, 1, 3):
        remote(c_slot, c_slot, c_sems.at[0], c_sems.at[1], (s, along_v[d])).start()

    @pl.when(home == v)
    def _():
        wait_bytes(f_recv.at[pl.ds(0, NS - 1)], f_sems.at[1])
        f_recv[my_slot] = f_send[...]

    @pl.when(home != v)
    def _():
        wait_bytes(f_recv, f_sems.at[1])

    lane_group = lax.broadcasted_iota(jnp.int32, (8, LANES), 1) // 32
    for t in range(TILES):
        halves = []
        for half in range(2):
            rows8 = jnp.zeros((8, LANES), F32)
            for m in range(NV):
                shift = (32 * (m - half)) % LANES
                got = f_recv[NV * t + m]
                got = pltpu.roll(got, shift, 1) if shift else got
                rows8 = jnp.where(lane_group == m, got, rows8)
            halves.append(rows8)
        p_now[t] = jnp.concatenate(halves, axis=0)
        p_start[t] = p_now[t]

    @pl.when(home == v)
    def _():
        wait_bytes(f_recv.at[pl.ds(0, NS - 1)], f_sems.at[0])

    @pl.when(home != v)
    def _():
        wait_bytes(f_recv, f_sems.at[0])

    def pick(tile):
        return jnp.where(core == 0, tile[:HALF], tile[HALF:K])

    def wait_alleles(cb):
        @pl.when(my_t // GROUP == cb)
        def _():
            wait_bytes(ag_all.at[pl.ds(0, 2 * GROUP - 1)], ag_recv.at[cb])

        @pl.when(my_t // GROUP != cb)
        def _():
            wait_bytes(ag_all.at[pl.ds(0, 2 * GROUP)], ag_recv.at[cb])

    def wait_alleles_sent():
        wait_bytes(ag_all.at[pl.ds(0, PIECES - 1)], ag_send.at[0])

    def tile_of(t):
        return jnp.concatenate(
            [ag_all[t][:HALF], ag_all[TILES + t][:HALF], jnp.zeros((ROWS - K, LANES), F32)],
            axis=0,
        )

    def em_step(step, carry):
        phase = lax.rem(step, 3)
        parity = lax.rem(step, 2)
        follows = jnp.logical_or(phase == 1, jnp.logical_and(phase == 0, step > 0))

        def prep_p(cb):
            @pl.when(follows)
            def _():
                wait_alleles(cb)
                for t in range(cb * GROUP, (cb + 1) * GROUP):
                    p_start[t] = p_now[t]
                    p_now[t] = tile_of(t)

            p = jnp.concatenate([p_now[t] for t in range(cb * GROUP, (cb + 1) * GROUP)], axis=1)
            ph, pm, pL = split3(p)
            pad = jnp.zeros((2 * ROWS, CB), F32)
            cols = pl.ds(cb * CB, CB)
            p_rows[:, cols] = jnp.concatenate([ph, pm, ph, pm, pL, ph, pad], axis=0).astype(BF16)
            p_three[...] = jnp.concatenate([ph, pm, pL], axis=0).astype(BF16)

        def stage_a(cb, rb, slot):
            cols = pl.ds(cb * CB, CB)
            rows = pl.ds(rb * RB, RB)
            expected = dot(q_cols[rows, :], p_rows[:, cols])
            for side, (counts, chance) in enumerate(
                ((alt_cnt, expected), (ref_cnt, 1.0 - expected))
            ):
                ratio = counts[rows, cols] * (1.0 / chance)
                w_buf[slot, 2 * side] = ratio.astype(BF16)
                high = w_buf[slot, 2 * side].astype(F32)
                w_buf[slot, 2 * side + 1] = (ratio - high).astype(BF16)

        def stage_b(cb, rb, slot, sums):
            rows = pl.ds(rb * RB, RB)
            q_part = q_rows[:, rows]
            p_part = p_three[...]
            sides = []
            props = []
            for side in range(2):
                high, low = w_buf[slot, 2 * side], w_buf[slot, 2 * side + 1]
                sides.append(dot(q_part, high) + dot(q_part, low))
                props.append(dot_t(p_part, high) + dot_t(p_part, low))
            prop = props[0] - props[1]
            prop_acc[:, rows] = prop if cb == 0 else prop_acc[:, rows] + prop
            return sides if sums is None else [sums[i] + sides[i] for i in range(2)]

        def send_pieces(cb, sums):
            alt, ref = [a[:ROWS] + a[ROWS : 2 * ROWS] + a[2 * ROWS :] for a in sums]
            for t in range(cb * CB // LANES, (cb + 1) * CB // LANES):
                lane = t * LANES - cb * CB
                for half in range(2):
                    piece = half * TILES + t
                    for row in range(HALF):
                        k = half * HALF + row
                        rs_send[piece, row] = jnp.concatenate(
                            [a[k : k + 1, lane : lane + LANES] for a in (alt, ref)], axis=0
                        )
                    first = ((t // 4) * 4 + t % 4) * 2 + half
                    other = ((t // 4 + 2) * 4 + (t + 2) % 4) * 2 + half
                    for target in (first, other):

                        @pl.when(s != target)
                        def _():
                            remote(
                                rs_send.at[piece],
                                rs_recv.at[parity, s],
                                rs_sems.at[2],
                                rs_sems.at[parity],
                                (target, v),
                            ).start()

        for cb in range(BLOCKS):
            prep_p(cb)
            sums = None
            stage_a(cb, 0, 0)
            stage_a(cb, 1, 1)
            for rb in range(SAMP // RB):
                if rb + 2 < SAMP // RB:
                    stage_a(cb, rb + 2, (rb + 2) % 4)
                sums = stage_b(cb, rb, rb % 4, sums)
            send_pieces(cb, sums)

        prop = prop_acc[:ROWS, :] + prop_acc[ROWS : 2 * ROWS, :] + prop_acc[2 * ROWS :, :]
        z_top[parity, v] = prop[:8]
        z_rest[parity, v] = prop[8:K]
        top_slot = z_top.at[parity, v]
        rest_slot = z_rest.at[parity, v]
        for d in (2, 1, 3):
            where = (s, along_v[d])
            remote(top_slot, top_slot, z_send.at[0], z_recv.at[parity], where).start()
            remote(rest_slot, rest_slot, z_send.at[1], y_recv.at[parity], where).start()

        def own_piece():
            wait_bytes(rs_recv.at[parity, pl.ds(0, NS - 1)], rs_sems.at[parity])
            rs_recv[parity, s] = rs_send[my_piece]
            sums = [rs_recv[parity, i] for i in range(NS)]
            while len(sums) > 1:
                sums = [sums[i] + sums[i + 1] for i in range(0, len(sums), 2)]
            alt_sum, ref_sum = sums[0][:, 0, :], sums[0][:, 1, :]
            old = pick(p_now[my_t])
            weighted = old * alt_sum
            new = clip_unit(weighted / (weighted + (1.0 - old) * ref_sum))

            @pl.when(step > 0)
            def _():
                wait_alleles_sent()

            r = old - pick(p_start[my_t])
            c = new - old - r
            squares = [jnp.sum(x * x, axis=0, keepdims=True) for x in (r, c)]
            squares = jnp.concatenate(squares, axis=0)
            ag_all[my_piece] = jnp.concatenate([new, squares, jnp.zeros((1, LANES), F32)], axis=0)
            ag_slot = ag_all.at[my_piece]
            for x, y in SERVED:
                for c in range(2):
                    if (x, y, c) != (0, 0, 0):
                        remote(
                            ag_slot, ag_slot, ag_send.at[0], ag_recv.at[my_t // GROUP], (moved(x, y, c), v)
                        ).start()

            @pl.when(phase == 1)
            def _():
                sp_out[...] = squares
                for d in (2, 1, 3):
                    for x, y in SERVED:
                        for c in range(2):
                            remote(
                                sp_out, sp_all.at[v, my_piece], sp_sems.at[0], sp_sems.at[1], (moved(x, y, c), along_v[d])
                            ).start()

        last_block = my_t // GROUP == BLOCKS - 1
        relaxed = jnp.logical_and(phase != 1, step < 3 * STEPS - 1)
        late = jnp.logical_and(last_block, relaxed)
        pl.when(jnp.logical_not(late))(own_piece)

        @pl.when(step == 0)
        def _():
            wait_bytes(c_all.at[pl.ds(0, NV - 1)], c_sems.at[1])
            twice_ref[...] = c_all[0] + c_all[1] + c_all[2] + c_all[3]
            wait_bytes(c_all.at[pl.ds(0, NV - 1)], c_sems.at[0])

        wait_bytes(z_top.at[parity, pl.ds(0, NV - 1)], z_recv.at[parity])
        wait_bytes(z_rest.at[parity, pl.ds(0, NV - 1)], y_recv.at[parity])
        q = q_now[...]
        top = z_top[parity, 0] + z_top[parity, 1] + z_top[parity, 2] + z_top[parity, 3]
        rest = z_rest[parity, 0] + z_rest[parity, 1] + z_rest[parity, 2] + z_rest[parity, 3]
        total = jnp.concatenate([top, rest, jnp.zeros((ROWS - K, SAMP), F32)], axis=0)
        twice = twice_ref[...]
        inner = jnp.sum(q * total, axis=0, keepdims=True)
        q_next = jnp.where(row_mask, clip_unit(q * (1.0 + (total - inner) / twice)), 0.0)

        @pl.when(phase == 1)
        def _():
            step_mix = q - q_start[...]
            curve_mix = q_next - q - step_mix
            row = [jnp.sum(a * a, axis=0, keepdims=True) for a in (step_mix, curve_mix)]
            row = jnp.concatenate(row, axis=0)
            part = row[:, :LANES]
            for t in range(1, TILES):
                part = part + row[:, t * LANES : (t + 1) * LANES]
            sq_q[s] = part

            sq_slot = sq_q.at[s]
            for x, y, c in SPREAD:
                if (x, y, c) != (0, 0, 0):
                    remote(
                        sq_slot, sq_slot, sq_sems.at[0], sq_sems.at[1], (moved(x, y, c), v)
                    ).start()

        @pl.when(phase != 1)
        def _():
            q_start[...] = q
            q_now[...] = q_next
            prep_q(q_next)

        pl.when(late)(own_piece)

        @pl.when(phase == 1)
        def _():
            for cb in range(BLOCKS):
                wait_alleles(cb)
            p_next = [tile_of(t) for t in range(TILES)]
            def alpha_of(sums):
                first = jnp.sum(sums[0:1], axis=1, keepdims=True)
                second = jnp.sum(sums[1:2], axis=1, keepdims=True)
                return jnp.maximum(1.0, jnp.sqrt(first / (second + NORM_EPS)))

            wait_bytes(sq_q.at[pl.ds(0, NS - 1)], sq_sems.at[1])
            sums = [sq_q[i] for i in range(NS)]
            while len(sums) > 1:
                sums = [sums[i] + sums[i + 1] for i in range(0, len(sums), 2)]
            alpha = alpha_of(sums[0])
            base = q_start[...]
            step_mix = q - base
            curve_mix = q_next - q - step_mix
            extra = clip_unit(base + 2.0 * alpha * step_mix + alpha * alpha * curve_mix)
            extra = jnp.where(row_mask, extra, 0.0)
            extra = extra / jnp.sum(extra, axis=0, keepdims=True)
            q_now[...] = extra
            prep_q(extra)

            for piece in range(PIECES):
                sp_all[v, piece] = ag_all[piece][HALF : HALF + 2]
            wait_bytes(sp_all.at[pl.ds(0, NV - 1)], sp_sems.at[1])
            sums = [jnp.sum(sp_all[i], axis=0) for i in range(NV)]
            alpha_p = alpha_of((sums[0] + sums[1]) + (sums[2] + sums[3]))
            for t in range(TILES):
                base_p = p_start[t]
                r = p_now[t] - base_p
                c = p_next[t] - p_now[t] - r
                extra_p = clip_unit(base_p + 2.0 * alpha_p * r + alpha_p * alpha_p * c)
                p_now[t] = jnp.where(row_mask, extra_p, 0.0)

            wait_bytes(sq_q.at[pl.ds(0, NS - 1)], sq_sems.at[0])
            wait_bytes(sp_all.at[pl.ds(0, NV - 1)], sp_sems.at[0])

        wait_bytes(z_top.at[parity, pl.ds(0, NV - 1)], z_send.at[0])
        wait_bytes(z_rest.at[parity, pl.ds(0, NV - 1)], z_send.at[1])
        wait_bytes(rs_send, rs_sems.at[2])
        wait_bytes(rs_send.at[pl.ds(0, PIECES - 1)], rs_sems.at[2])
        return carry

    lax.fori_loop(0, 3 * STEPS, em_step, 0)
    mix_ref[...] = q_now[:K, :]
    for cb in range(BLOCKS):
        wait_alleles(cb)
    for t in range(TILES):
        allele_ref[:, t * LANES : (t + 1) * LANES] = tile_of(t)[:K]
    wait_alleles_sent()


def finish(mix_in, allele_in, mix_out, allele_out):
    mix_out[...] = mix_in[...]
    allele_out[...] = allele_in[...]


def local(genotypes, observed, proportions, frequencies):
    vmem = pl.BlockSpec(memory_space=pltpu.VMEM)
    hbm = pl.BlockSpec(memory_space=pl.ANY)
    dma = pltpu.SemaphoreType.DMA
    outs = pl.pallas_call(
        kernel,
        name="em",
        out_shape=(
            jax.ShapeDtypeStruct((K, SAMP), F32),
            jax.ShapeDtypeStruct((K, VARS), F32),
        ),
        in_specs=[hbm, hbm, hbm, hbm],
        out_specs=(vmem, vmem),
        scratch_shapes=[
            pltpu.VMEM((SAMP, VARS), jnp.int32),
            pltpu.VMEM((SAMP, VARS), jnp.int32),
            pltpu.VMEM((SAMP, VARS), F32),
            pltpu.VMEM((SAMP, VARS), F32),
            pltpu.VMEM((ROWS, SAMP), F32),
            pltpu.VMEM((3 * ROWS, SAMP), F32),
            pltpu.VMEM((ROWS, SAMP), F32),
            pltpu.VMEM((ROWS, SAMP), F32),
            pltpu.VMEM((TILES, ROWS, LANES), F32),
            pltpu.VMEM((TILES, ROWS, LANES), F32),
            pltpu.VMEM((SAMP, LANES), BF16),
            pltpu.VMEM((LANES, VARS), BF16),
            pltpu.VMEM((3 * ROWS, SAMP), BF16),
            pltpu.VMEM((3 * ROWS, CB), BF16),
            pltpu.VMEM((4, 4, RB, CB), BF16),
            pltpu.VMEM((K, SAMP), F32),
            pltpu.VMEM((K, 32), F32),
            pltpu.VMEM((8, LANES), F32),
            pltpu.VMEM((NS, 8, LANES), F32),
            pltpu.VMEM((PIECES, HALF, 2, LANES), F32),
            pltpu.VMEM((2, NS, HALF, 2, LANES), F32),
            pltpu.VMEM((PIECES, 8, LANES), F32),
            pltpu.VMEM((2, NV, 8, SAMP), F32),
            pltpu.VMEM((2, NV, K - 8, SAMP), F32),
            pltpu.VMEM((NV, 1, SAMP), F32),
            pltpu.VMEM((1, SAMP), F32),
            pltpu.VMEM((NS, 2, LANES), F32),
            pltpu.VMEM((NV, PIECES, 2, LANES), F32),
            pltpu.VMEM((2, LANES), F32),
            dma((2, CHUNKS)),
            dma((2,)),
            dma((2,)),
            dma((3,)),
            dma((1,)),
            dma((BLOCKS,)),
            dma((2,)),
            dma((2,)),
            dma((2,)),
            dma((2,)),
            dma((2,)),
            dma((2,)),
        ],
        compiler_params=pltpu.CompilerParams(
            collective_id=0, has_side_effects=True, vmem_limit_bytes=60 * 1024 * 1024
        ),
    )(genotypes, observed, proportions, frequencies)
    return pl.pallas_call(
        finish,
        name="finish",
        out_shape=(
            jax.ShapeDtypeStruct((K, SAMP), F32),
            jax.ShapeDtypeStruct((K, VARS), F32),
        ),
        in_specs=[vmem, vmem],
        out_specs=(vmem, vmem),
    )(*outs)


def solution(mesh):
    placed = (P("samp", "var"), P("samp", "var"), P(None, "samp"), P(None, ("samp", "var")))
    return jax.shard_map(
        local,
        mesh=mesh,
        in_specs=placed,
        out_specs=(P(None, "samp"), P(None, "var")),
        check_vma=False,
    )
```

```python
import jax
import jax.numpy as jnp
from jax import lax
from jax.experimental import pallas as pl
from jax.experimental.pallas import tpu as pltpu
from jax.sharding import PartitionSpec as P

STEPS = 2
CLIP_LOW = 1e-05
NORM_EPS = 1e-10
MESH = pl.DeviceIdType.MESH

K = 10
ROWS = 16
NS = 32
NV = 4
SAMP = 1024
VARS = 1024
LANES = 128
TILES = VARS // LANES
HALF = K // 2
PIECES = 2 * TILES
SERVED = ((2, 0), (1, 1), (1, 3), (3, 0), (1, 0), (0, 3), (0, 1), (0, 0))
SPREAD = sorted(
    ((x, y, c) for x in range(4) for y in range(4) for c in range(2)),
    key=lambda d: -(min(d[0], 4 - d[0]) + min(d[1], 4 - d[1])),
)
RB = 256
CB = 256
BLOCKS = VARS // CB
GROUP = CB // LANES
CHUNK = 128
CHUNKS = SAMP // CHUNK

F32 = jnp.float32
BF16 = jnp.bfloat16


def clip_unit(values):
    return jnp.clip(values, CLIP_LOW, 1.0 - CLIP_LOW)


def split3(values):
    high = values.astype(BF16).astype(F32)
    rest = values - high
    mid = rest.astype(BF16).astype(F32)
    low = (rest - mid).astype(BF16).astype(F32)
    return high, mid, low


def dot(a, b):
    return lax.dot_general(
        a, b, (((1,), (0,)), ((), ())), preferred_element_type=F32
    )


def dot_t(a, b):
    return lax.dot_general(
        a, b, (((1,), (1,)), ((), ())), preferred_element_type=F32
    )


def kernel(
    geno_hbm,
    seen_hbm,
    props_ref,
    freqs_ref,
    mix_ref,
    allele_ref,
    geno_buf,
    seen_buf,
    alt_cnt,
    ref_cnt,
    count_acc,
    prop_acc,
    q_now,
    q_start,
    p_now,
    p_start,
    q_cols,
    p_rows,
    q_rows,
    p_three,
    w_buf,
    props_buf,
    freqs_buf,
    f_send,
    f_recv,
    rs_send,
    rs_recv,
    ag_all,
    z_top,
    z_rest,
    c_all,
    twice_ref,
    sq_q,
    sp_all,
    sp_out,
    load_sem,
    small_sem,
    f_sems,
    rs_sems,
    ag_send,
    ag_recv,
    z_send,
    z_recv,
    y_recv,
    c_sems,
    sq_sems,
    sp_sems,
):
    s = lax.axis_index("samp")
    v = lax.axis_index("var")
    chip_x = s // 8
    chip_y = lax.rem(s // 2, 4)
    core = lax.rem(s, 2)
    my_t = lax.rem(chip_x, 2) * 4 + lax.rem(chip_y + 2 * (chip_x // 2), 4)
    my_piece = core * TILES + my_t

    along_x = [lax.rem(chip_x + d, 4) * 8 for d in range(4)]
    along_y = [lax.rem(chip_y + d, 4) * 2 for d in range(4)]
    cores = (core, 1 - core)
    along_v = [lax.rem(v + d, NV) for d in range(NV)]

    def moved(x, y, c):
        return along_x[x] + along_y[y] + cores[c]

    home = s // TILES

    def remote(src, dst, send_sem, recv_sem, where):
        return pltpu.make_async_remote_copy(
            src_ref=src,
            dst_ref=dst,
            send_sem=send_sem,
            recv_sem=recv_sem,
            device_id=where,
            device_id_type=MESH,
        )

    def wait_bytes(ref, sem):
        pltpu.make_async_copy(ref, ref, sem).wait()

    def load(chunk):
        rows = pl.ds(chunk * CHUNK, CHUNK)
        return (
            pltpu.make_async_copy(geno_hbm.at[rows], geno_buf.at[rows], load_sem.at[0, chunk]),
            pltpu.make_async_copy(seen_hbm.at[rows], seen_buf.at[rows], load_sem.at[1, chunk]),
        )

    small = (
        pltpu.make_async_copy(freqs_ref, freqs_buf, small_sem.at[0]),
        pltpu.make_async_copy(props_ref, props_buf, small_sem.at[1]),
    )
    for copy in small:
        copy.start()
    for chunk in range(CHUNKS):
        for copy in load(chunk):
            copy.start()

    barrier = pltpu.get_barrier_semaphore()

    def greet(where):
        pl.semaphore_signal(barrier, inc=1, device_id=where, device_id_type=MESH)

    def greet_samp(d, carry):
        greet((lax.rem(s + d, NS), v))
        return carry

    def greet_var(d, carry):
        greet((s, lax.rem(v + d, NV)))
        return carry

    def greet_source(i, carry):
        far_s = v * TILES + i // NV
        far_v = lax.rem(i, NV)

        @pl.when(jnp.logical_or(far_s != s, far_v != v))
        def _():
            greet((far_s, far_v))

        return carry

    lax.fori_loop(0, NS, greet_source, 0)
    lax.fori_loop(1, NV, greet_var, 0)
    lax.fori_loop(1, NS, greet_samp, 0)

    row_ids = lax.broadcasted_iota(jnp.int32, (ROWS, 1), 0)
    row_mask = row_ids < K

    small[0].wait()
    block = freqs_buf[...]
    tail = jnp.concatenate([block[8:K], jnp.zeros((ROWS - K, 32), F32)], axis=0)
    f_send[...] = jnp.concatenate([block[:8], tail, jnp.zeros((8, 64), F32)], axis=1)

    @pl.when(home == v)
    def _():
        pl.semaphore_wait(barrier, NS - 1 + NV - 1 + NS - 1)

    @pl.when(home != v)
    def _():
        pl.semaphore_wait(barrier, NS - 1 + NV - 1 + NS)

    my_slot = NV * lax.rem(s, TILES) + v

    for x, y, c in SPREAD:
        copy = remote(f_send, f_recv.at[my_slot], f_sems.at[0], f_sems.at[1], (moved(x, y, c), home))
        if (x, y, c) != (0, 0, 0):
            copy.start()
        else:
            pl.when(home != v)(copy.start)

    small[1].wait()
    q_now[...] = jnp.concatenate([props_buf[...], jnp.zeros((ROWS - K, SAMP), F32)], axis=0)

    def prep_q(q):
        qh, qm, ql = split3(q)
        pad = jnp.zeros((2 * ROWS, SAMP), F32)
        q_cols[...] = jnp.concatenate([qh, qh, qm, qm, qh, ql, pad], axis=0).T.astype(BF16)
        q_rows[...] = jnp.concatenate([qh, qm, ql], axis=0).astype(BF16)

    prep_q(q_now[...])

    count_w = jnp.full((ROWS, VARS), 2.0, BF16)

    def convert(chunk):
        for copy in load(chunk):
            copy.wait()
        rows = pl.ds(chunk * CHUNK, CHUNK)
        seen = seen_buf[rows, :].astype(F32)
        alt = seen * geno_buf[rows, :].astype(F32)
        alt_cnt[rows, :] = alt
        ref_cnt[rows, :] = 2.0 * seen - alt
        count_acc[:, rows] = dot_t(count_w, seen.astype(BF16))

    for chunk in range(CHUNKS):
        convert(chunk)

    c_all[v] = count_acc[:1, :]
    c_slot = c_all.at[v]
    for d in (2, 1, 3):
        remote(c_slot, c_slot, c_sems.at[0], c_sems.at[1], (s, along_v[d])).start()

    @pl.when(home == v)
    def _():
        wait_bytes(f_recv.at[pl.ds(0, NS - 1)], f_sems.at[1])
        f_recv[my_slot] = f_send[...]

    @pl.when(home != v)
    def _():
        wait_bytes(f_recv, f_sems.at[1])

    lane_group = lax.broadcasted_iota(jnp.int32, (8, LANES), 1) // 32
    for t in range(TILES):
        halves = []
        for half in range(2):
            rows8 = jnp.zeros((8, LANES), F32)
            for m in range(NV):
                shift = (32 * (m - half)) % LANES
                got = f_recv[NV * t + m]
                got = pltpu.roll(got, shift, 1) if shift else got
                rows8 = jnp.where(lane_group == m, got, rows8)
            halves.append(rows8)
        p_now[t] = jnp.concatenate(halves, axis=0)
        p_start[t] = p_now[t]

    @pl.when(home == v)
    def _():
        wait_bytes(f_recv.at[pl.ds(0, NS - 1)], f_sems.at[0])

    @pl.when(home != v)
    def _():
        wait_bytes(f_recv, f_sems.at[0])

    def pick(tile):
        return jnp.where(core == 0, tile[:HALF], tile[HALF:K])

    def wait_alleles(cb):
        @pl.when(my_t // GROUP == cb)
        def _():
            wait_bytes(ag_all.at[pl.ds(0, 2 * GROUP - 1)], ag_recv.at[cb])

        @pl.when(my_t // GROUP != cb)
        def _():
            wait_bytes(ag_all.at[pl.ds(0, 2 * GROUP)], ag_recv.at[cb])

    def wait_alleles_sent():
        wait_bytes(ag_all.at[pl.ds(0, PIECES - 1)], ag_send.at[0])

    def tile_of(t):
        return jnp.concatenate(
            [ag_all[t][:HALF], ag_all[TILES + t][:HALF], jnp.zeros((ROWS - K, LANES), F32)],
            axis=0,
        )

    def em_step(step, carry):
        phase = lax.rem(step, 3)
        parity = lax.rem(step, 2)
        follows = jnp.logical_or(phase == 1, jnp.logical_and(phase == 0, step > 0))

        def prep_p(cb):
            @pl.when(follows)
            def _():
                wait_alleles(cb)
                for t in range(cb * GROUP, (cb + 1) * GROUP):
                    p_start[t] = p_now[t]
                    p_now[t] = tile_of(t)

            p = jnp.concatenate([p_now[t] for t in range(cb * GROUP, (cb + 1) * GROUP)], axis=1)
            ph, pm, pL = split3(p)
            pad = jnp.zeros((2 * ROWS, CB), F32)
            cols = pl.ds(cb * CB, CB)
            p_rows[:, cols] = jnp.concatenate([ph, pm, ph, pm, pL, ph, pad], axis=0).astype(BF16)
            p_three[...] = jnp.concatenate([ph, pm, pL], axis=0).astype(BF16)

        def stage_a(cb, rb, slot):
            cols = pl.ds(cb * CB, CB)
            rows = pl.ds(rb * RB, RB)
            expected = dot(q_cols[rows, :], p_rows[:, cols])
            ratios = []
            for side, (counts, chance) in enumerate(
                ((alt_cnt, expected), (ref_cnt, 1.0 - expected))
            ):
                ratios.append(counts[rows, cols] * (1.0 / chance))
            ratios.append(ratios[0] - ratios[1])
            for side, ratio in enumerate(ratios):
                w_buf[slot, 2 * side] = ratio.astype(BF16)
                high = w_buf[slot, 2 * side].astype(F32)
                w_buf[slot, 2 * side + 1] = (ratio - high).astype(BF16)

        def stage_b(cb, rb, slot, sums):
            rows = pl.ds(rb * RB, RB)
            q_part = q_rows[:, rows]
            p_part = p_three[...]
            sides = []
            for side in range(2):
                high, low = w_buf[slot, 2 * side], w_buf[slot, 2 * side + 1]
                sides.append(dot(q_part, high) + dot(q_part, low))
            prop = dot_t(p_part, w_buf[slot, 4]) + dot_t(p_part, w_buf[slot, 5])
            prop_acc[:, rows] = prop if cb == 0 else prop_acc[:, rows] + prop
            return sides if sums is None else [sums[i] + sides[i] for i in range(2)]

        def send_pieces(cb, sums):
            alt, ref = [a[:ROWS] + a[ROWS : 2 * ROWS] + a[2 * ROWS :] for a in sums]
            for t in range(cb * CB // LANES, (cb + 1) * CB // LANES):
                lane = t * LANES - cb * CB
                for half in range(2):
                    piece = half * TILES + t
                    for row in range(HALF):
                        k = half * HALF + row
                        rs_send[piece, row] = jnp.concatenate(
                            [a[k : k + 1, lane : lane + LANES] for a in (alt, ref)], axis=0
                        )
                    first = ((t // 4) * 4 + t % 4) * 2 + half
                    other = ((t // 4 + 2) * 4 + (t + 2) % 4) * 2 + half
                    for target in (first, other):

                        @pl.when(s != target)
                        def _():
                            remote(
                                rs_send.at[piece],
                                rs_recv.at[parity, s],
                                rs_sems.at[2],
                                rs_sems.at[parity],
                                (target, v),
                            ).start()

        for cb in range(BLOCKS):
            prep_p(cb)
            sums = None
            stage_a(cb, 0, 0)
            stage_a(cb, 1, 1)
            for rb in range(SAMP // RB):
                if rb + 2 < SAMP // RB:
                    stage_a(cb, rb + 2, (rb + 2) % 4)
                sums = stage_b(cb, rb, rb % 4, sums)
            send_pieces(cb, sums)

        prop = prop_acc[:ROWS, :] + prop_acc[ROWS : 2 * ROWS, :] + prop_acc[2 * ROWS :, :]
        z_top[parity, v] = prop[:8]
        z_rest[parity, v] = prop[8:K]
        top_slot = z_top.at[parity, v]
        rest_slot = z_rest.at[parity, v]
        for d in (2, 1, 3):
            where = (s, along_v[d])
            remote(top_slot, top_slot, z_send.at[0], z_recv.at[parity], where).start()
            remote(rest_slot, rest_slot, z_send.at[1], y_recv.at[parity], where).start()

        def own_piece():
            wait_bytes(rs_recv.at[parity, pl.ds(0, NS - 1)], rs_sems.at[parity])
            rs_recv[parity, s] = rs_send[my_piece]
            sums = [rs_recv[parity, i] for i in range(NS)]
            while len(sums) > 1:
                sums = [sums[i] + sums[i + 1] for i in range(0, len(sums), 2)]
            alt_sum, ref_sum = sums[0][:, 0, :], sums[0][:, 1, :]
            old = pick(p_now[my_t])
            weighted = old * alt_sum
            new = clip_unit(weighted / (weighted + (1.0 - old) * ref_sum))

            @pl.when(step > 0)
            def _():
                wait_alleles_sent()

            r = old - pick(p_start[my_t])
            c = new - old - r
            squares = [jnp.sum(x * x, axis=0, keepdims=True) for x in (r, c)]
            squares = jnp.concatenate(squares, axis=0)
            ag_all[my_piece] = jnp.concatenate([new, squares, jnp.zeros((1, LANES), F32)], axis=0)
            ag_slot = ag_all.at[my_piece]
            for x, y in SERVED:
                for c in range(2):
                    if (x, y, c) != (0, 0, 0):
                        remote(
                            ag_slot, ag_slot, ag_send.at[0], ag_recv.at[my_t // GROUP], (moved(x, y, c), v)
                        ).start()

            @pl.when(phase == 1)
            def _():
                sp_out[...] = squares
                for d in (2, 1, 3):
                    for x, y in SERVED:
                        for c in range(2):
                            remote(
                                sp_out, sp_all.at[v, my_piece], sp_sems.at[0], sp_sems.at[1], (moved(x, y, c), along_v[d])
                            ).start()

        last_block = my_t // GROUP == BLOCKS - 1
        relaxed = jnp.logical_and(phase != 1, step < 3 * STEPS - 1)
        late = jnp.logical_and(last_block, relaxed)
        pl.when(jnp.logical_not(late))(own_piece)

        @pl.when(step == 0)
        def _():
            wait_bytes(c_all.at[pl.ds(0, NV - 1)], c_sems.at[1])
            twice_ref[...] = c_all[0] + c_all[1] + c_all[2] + c_all[3]
            wait_bytes(c_all.at[pl.ds(0, NV - 1)], c_sems.at[0])

        wait_bytes(z_top.at[parity, pl.ds(0, NV - 1)], z_recv.at[parity])
        wait_bytes(z_rest.at[parity, pl.ds(0, NV - 1)], y_recv.at[parity])
        q = q_now[...]
        top = z_top[parity, 0] + z_top[parity, 1] + z_top[parity, 2] + z_top[parity, 3]
        rest = z_rest[parity, 0] + z_rest[parity, 1] + z_rest[parity, 2] + z_rest[parity, 3]
        total = jnp.concatenate([top, rest, jnp.zeros((ROWS - K, SAMP), F32)], axis=0)
        twice = twice_ref[...]
        inner = jnp.sum(q * total, axis=0, keepdims=True)
        q_next = jnp.where(row_mask, clip_unit(q * (1.0 + (total - inner) / twice)), 0.0)

        @pl.when(phase == 1)
        def _():
            step_mix = q - q_start[...]
            curve_mix = q_next - q - step_mix
            row = [jnp.sum(a * a, axis=0, keepdims=True) for a in (step_mix, curve_mix)]
            row = jnp.concatenate(row, axis=0)
            part = row[:, :LANES]
            for t in range(1, TILES):
                part = part + row[:, t * LANES : (t + 1) * LANES]
            sq_q[s] = part

            sq_slot = sq_q.at[s]
            for x, y, c in SPREAD:
                if (x, y, c) != (0, 0, 0):
                    remote(
                        sq_slot, sq_slot, sq_sems.at[0], sq_sems.at[1], (moved(x, y, c), v)
                    ).start()

        @pl.when(phase != 1)
        def _():
            q_start[...] = q
            q_now[...] = q_next
            prep_q(q_next)

        pl.when(late)(own_piece)

        @pl.when(phase == 1)
        def _():
            for cb in range(BLOCKS):
                wait_alleles(cb)
            p_next = [tile_of(t) for t in range(TILES)]
            def alpha_of(sums):
                first = jnp.sum(sums[0:1], axis=1, keepdims=True)
                second = jnp.sum(sums[1:2], axis=1, keepdims=True)
                return jnp.maximum(1.0, jnp.sqrt(first / (second + NORM_EPS)))

            wait_bytes(sq_q.at[pl.ds(0, NS - 1)], sq_sems.at[1])
            sums = [sq_q[i] for i in range(NS)]
            while len(sums) > 1:
                sums = [sums[i] + sums[i + 1] for i in range(0, len(sums), 2)]
            alpha = alpha_of(sums[0])
            base = q_start[...]
            step_mix = q - base
            curve_mix = q_next - q - step_mix
            extra = clip_unit(base + 2.0 * alpha * step_mix + alpha * alpha * curve_mix)
            extra = jnp.where(row_mask, extra, 0.0)
            extra = extra / jnp.sum(extra, axis=0, keepdims=True)
            q_now[...] = extra
            prep_q(extra)

            for piece in range(PIECES):
                sp_all[v, piece] = ag_all[piece][HALF : HALF + 2]
            wait_bytes(sp_all.at[pl.ds(0, NV - 1)], sp_sems.at[1])
            sums = [jnp.sum(sp_all[i], axis=0) for i in range(NV)]
            alpha_p = alpha_of((sums[0] + sums[1]) + (sums[2] + sums[3]))
            for t in range(TILES):
                base_p = p_start[t]
                r = p_now[t] - base_p
                c = p_next[t] - p_now[t] - r
                extra_p = clip_unit(base_p + 2.0 * alpha_p * r + alpha_p * alpha_p * c)
                p_now[t] = jnp.where(row_mask, extra_p, 0.0)

            wait_bytes(sq_q.at[pl.ds(0, NS - 1)], sq_sems.at[0])
            wait_bytes(sp_all.at[pl.ds(0, NV - 1)], sp_sems.at[0])

        wait_bytes(z_top.at[parity, pl.ds(0, NV - 1)], z_send.at[0])
        wait_bytes(z_rest.at[parity, pl.ds(0, NV - 1)], z_send.at[1])
        wait_bytes(rs_send, rs_sems.at[2])
        wait_bytes(rs_send.at[pl.ds(0, PIECES - 1)], rs_sems.at[2])
        return carry

    lax.fori_loop(0, 3 * STEPS, em_step, 0)
    mix_ref[...] = q_now[:K, :]
    for cb in range(BLOCKS):
        wait_alleles(cb)
    for t in range(TILES):
        allele_ref[:, t * LANES : (t + 1) * LANES] = tile_of(t)[:K]
    wait_alleles_sent()


def finish(mix_in, allele_in, mix_out, allele_out):
    mix_out[...] = mix_in[...]
    allele_out[...] = allele_in[...]


def local(genotypes, observed, proportions, frequencies):
    vmem = pl.BlockSpec(memory_space=pltpu.VMEM)
    hbm = pl.BlockSpec(memory_space=pl.ANY)
    dma = pltpu.SemaphoreType.DMA
    outs = pl.pallas_call(
        kernel,
        name="em",
        out_shape=(
            jax.ShapeDtypeStruct((K, SAMP), F32),
            jax.ShapeDtypeStruct((K, VARS), F32),
        ),
        in_specs=[hbm, hbm, hbm, hbm],
        out_specs=(vmem, vmem),
        scratch_shapes=[
            pltpu.VMEM((SAMP, VARS), jnp.int32),
            pltpu.VMEM((SAMP, VARS), jnp.int32),
            pltpu.VMEM((SAMP, VARS), F32),
            pltpu.VMEM((SAMP, VARS), F32),
            pltpu.VMEM((ROWS, SAMP), F32),
            pltpu.VMEM((3 * ROWS, SAMP), F32),
            pltpu.VMEM((ROWS, SAMP), F32),
            pltpu.VMEM((ROWS, SAMP), F32),
            pltpu.VMEM((TILES, ROWS, LANES), F32),
            pltpu.VMEM((TILES, ROWS, LANES), F32),
            pltpu.VMEM((SAMP, LANES), BF16),
            pltpu.VMEM((LANES, VARS), BF16),
            pltpu.VMEM((3 * ROWS, SAMP), BF16),
            pltpu.VMEM((3 * ROWS, CB), BF16),
            pltpu.VMEM((4, 6, RB, CB), BF16),
            pltpu.VMEM((K, SAMP), F32),
            pltpu.VMEM((K, 32), F32),
            pltpu.VMEM((8, LANES), F32),
            pltpu.VMEM((NS, 8, LANES), F32),
            pltpu.VMEM((PIECES, HALF, 2, LANES), F32),
            pltpu.VMEM((2, NS, HALF, 2, LANES), F32),
            pltpu.VMEM((PIECES, 8, LANES), F32),
            pltpu.VMEM((2, NV, 8, SAMP), F32),
            pltpu.VMEM((2, NV, K - 8, SAMP), F32),
            pltpu.VMEM((NV, 1, SAMP), F32),
            pltpu.VMEM((1, SAMP), F32),
            pltpu.VMEM((NS, 2, LANES), F32),
            pltpu.VMEM((NV, PIECES, 2, LANES), F32),
            pltpu.VMEM((2, LANES), F32),
            dma((2, CHUNKS)),
            dma((2,)),
            dma((2,)),
            dma((3,)),
            dma((1,)),
            dma((BLOCKS,)),
            dma((2,)),
            dma((2,)),
            dma((2,)),
            dma((2,)),
            dma((2,)),
            dma((2,)),
        ],
        compiler_params=pltpu.CompilerParams(
            collective_id=0, has_side_effects=True, vmem_limit_bytes=60 * 1024 * 1024
        ),
    )(genotypes, observed, proportions, frequencies)
    return pl.pallas_call(
        finish,
        name="finish",
        out_shape=(
            jax.ShapeDtypeStruct((K, SAMP), F32),
            jax.ShapeDtypeStruct((K, VARS), F32),
        ),
        in_specs=[vmem, vmem],
        out_specs=(vmem, vmem),
    )(*outs)


def solution(mesh):
    placed = (P("samp", "var"), P("samp", "var"), P(None, "samp"), P(None, ("samp", "var")))
    return jax.shard_map(
        local,
        mesh=mesh,
        in_specs=placed,
        out_specs=(P(None, "samp"), P(None, "var")),
        check_vma=False,
    )
```

```python
import jax
import jax.numpy as jnp
from jax import lax
from jax.experimental import pallas as pl
from jax.experimental.pallas import tpu as pltpu
from jax.sharding import PartitionSpec as P

STEPS = 2
CLIP_LOW = 1e-05
NORM_EPS = 1e-10
MESH = pl.DeviceIdType.MESH

K = 10
ROWS = 16
NS = 32
NV = 4
SAMP = 1024
VARS = 1024
LANES = 128
TILES = VARS // LANES
HALF = K // 2
PIECES = 2 * TILES
SERVED = ((2, 0), (1, 1), (1, 3), (3, 0), (1, 0), (0, 3), (0, 1), (0, 0))
SPREAD = sorted(
    ((x, y, c) for x in range(4) for y in range(4) for c in range(2)),
    key=lambda d: -(min(d[0], 4 - d[0]) + min(d[1], 4 - d[1])),
)
RB = 256
CB = 256
BLOCKS = VARS // CB
GROUP = CB // LANES
CHUNK = 128
CHUNKS = SAMP // CHUNK

F32 = jnp.float32
BF16 = jnp.bfloat16
FAR = sorted(
    ((x, y, c, d) for x, y in SERVED for c in range(2) for d in range(1, NV)),
    key=lambda e: -sum(min(a, 4 - a) for a in (e[0], e[1], e[3])),
)


def clip_unit(values):
    return jnp.clip(values, CLIP_LOW, 1.0 - CLIP_LOW)


def split3(values):
    high = values.astype(BF16).astype(F32)
    rest = values - high
    mid = rest.astype(BF16).astype(F32)
    low = (rest - mid).astype(BF16).astype(F32)
    return high, mid, low


def dot(a, b):
    return lax.dot_general(
        a, b, (((1,), (0,)), ((), ())), preferred_element_type=F32
    )


def dot_t(a, b):
    return lax.dot_general(
        a, b, (((1,), (1,)), ((), ())), preferred_element_type=F32
    )


def kernel(
    geno_hbm,
    seen_hbm,
    props_ref,
    freqs_ref,
    mix_ref,
    allele_ref,
    geno_buf,
    seen_buf,
    alt_cnt,
    ref_cnt,
    count_acc,
    prop_acc,
    q_now,
    q_start,
    p_now,
    p_start,
    q_cols,
    p_rows,
    q_rows,
    p_three,
    w_buf,
    props_buf,
    freqs_buf,
    f_send,
    f_recv,
    rs_send,
    rs_recv,
    ag_all,
    z_top,
    z_rest,
    c_all,
    twice_ref,
    sq_q,
    sp_all,
    sp_out,
    load_sem,
    small_sem,
    f_sems,
    rs_sems,
    ag_send,
    ag_recv,
    z_send,
    z_recv,
    y_recv,
    c_sems,
    sq_sems,
    sp_sems,
):
    s = lax.axis_index("samp")
    v = lax.axis_index("var")
    chip_x = s // 8
    chip_y = lax.rem(s // 2, 4)
    core = lax.rem(s, 2)
    my_t = lax.rem(chip_x, 2) * 4 + lax.rem(chip_y + 2 * (chip_x // 2), 4)
    my_piece = core * TILES + my_t

    along_x = [lax.rem(chip_x + d, 4) * 8 for d in range(4)]
    along_y = [lax.rem(chip_y + d, 4) * 2 for d in range(4)]
    cores = (core, 1 - core)
    along_v = [lax.rem(v + d, NV) for d in range(NV)]

    def moved(x, y, c):
        return along_x[x] + along_y[y] + cores[c]

    home = s // TILES

    def remote(src, dst, send_sem, recv_sem, where):
        return pltpu.make_async_remote_copy(
            src_ref=src,
            dst_ref=dst,
            send_sem=send_sem,
            recv_sem=recv_sem,
            device_id=where,
            device_id_type=MESH,
        )

    def wait_bytes(ref, sem):
        pltpu.make_async_copy(ref, ref, sem).wait()

    def load(chunk):
        rows = pl.ds(chunk * CHUNK, CHUNK)
        return (
            pltpu.make_async_copy(geno_hbm.at[rows], geno_buf.at[rows], load_sem.at[0, chunk]),
            pltpu.make_async_copy(seen_hbm.at[rows], seen_buf.at[rows], load_sem.at[1, chunk]),
        )

    barrier = pltpu.get_barrier_semaphore()

    def greet(where):
        pl.semaphore_signal(barrier, inc=1, device_id=where, device_id_type=MESH)

    first_source = v * TILES
    for i in range(NS):
        source = (first_source + i // NV, i % NV)

        @pl.when(jnp.logical_or(source[0] != s, v != source[1]))
        def _():
            greet(source)

    for x, y, c in SPREAD:
        if (x, y, c) != (0, 0, 0):
            greet((moved(x, y, c), v))
    for d in (2, 1, 3):
        greet((s, along_v[d]))

    small = (
        pltpu.make_async_copy(freqs_ref, freqs_buf, small_sem.at[0]),
        pltpu.make_async_copy(props_ref, props_buf, small_sem.at[1]),
    )
    for copy in small:
        copy.start()
    for chunk in range(CHUNKS):
        for copy in load(chunk):
            copy.start()

    row_ids = lax.broadcasted_iota(jnp.int32, (ROWS, 1), 0)
    row_mask = row_ids < K

    small[0].wait()
    block = freqs_buf[...]
    tail = jnp.concatenate([block[8:K], jnp.zeros((12 - K, 32), F32)], axis=0)
    f_send[...] = jnp.concatenate([block[:4], block[4:8], tail, jnp.zeros((4, 32), F32)], axis=1)

    @pl.when(home == v)
    def _():
        pl.semaphore_wait(barrier, NS - 1 + NV - 1 + NS - 1)

    @pl.when(home != v)
    def _():
        pl.semaphore_wait(barrier, NS - 1 + NV - 1 + NS)

    my_slot = NV * lax.rem(s, TILES) + v

    for x, y, c in SPREAD:
        copy = remote(f_send, f_recv.at[my_slot], f_sems.at[0], f_sems.at[1], (moved(x, y, c), home))
        if (x, y, c) != (0, 0, 0):
            copy.start()
        else:
            pl.when(home != v)(copy.start)

    small[1].wait()
    q_now[...] = jnp.concatenate([props_buf[...], jnp.zeros((ROWS - K, SAMP), F32)], axis=0)

    def prep_q(q):
        qh, qm, ql = split3(q)
        pad = jnp.zeros((2 * ROWS, SAMP), F32)
        q_cols[...] = jnp.concatenate([qh, qh, qm, qm, qh, ql, pad], axis=0).T.astype(BF16)
        q_rows[...] = jnp.concatenate([qh, qm, ql], axis=0).astype(BF16)

    prep_q(q_now[...])

    count_w = jnp.full((ROWS, VARS), 2.0, BF16)

    def convert(chunk):
        for copy in load(chunk):
            copy.wait()
        rows = pl.ds(chunk * CHUNK, CHUNK)
        seen = seen_buf[rows, :].astype(F32)
        alt = seen * geno_buf[rows, :].astype(F32)
        alt_cnt[rows, :] = alt
        ref_cnt[rows, :] = 2.0 * seen - alt
        count_acc[:, rows] = dot_t(count_w, seen.astype(BF16))

    for chunk in range(CHUNKS):
        convert(chunk)

    c_all[v] = count_acc[:1, :]
    c_slot = c_all.at[v]
    for d in (2, 1, 3):
        remote(c_slot, c_slot, c_sems.at[0], c_sems.at[1], (s, along_v[d])).start()

    @pl.when(home == v)
    def _():
        wait_bytes(f_recv.at[pl.ds(0, NS - 1)], f_sems.at[1])
        f_recv[my_slot] = f_send[...]

    @pl.when(home != v)
    def _():
        wait_bytes(f_recv, f_sems.at[1])

    lane_group = lax.broadcasted_iota(jnp.int32, (4, LANES), 1) // 32
    for t in range(TILES):
        groups = []
        for group in range(3):
            rows4 = jnp.zeros((4, LANES), F32)
            for m in range(NV):
                shift = (32 * (m - group)) % LANES
                got = f_recv[NV * t + m]
                got = pltpu.roll(got, shift, 1) if shift else got
                rows4 = jnp.where(lane_group == m, got, rows4)
            groups.append(rows4)
        p_now[t] = jnp.concatenate(groups + [jnp.zeros((4, LANES), F32)], axis=0)
        p_start[t] = p_now[t]

    @pl.when(home == v)
    def _():
        wait_bytes(f_recv.at[pl.ds(0, NS - 1)], f_sems.at[0])

    @pl.when(home != v)
    def _():
        wait_bytes(f_recv, f_sems.at[0])

    def pick(tile):
        return jnp.where(core == 0, tile[:HALF], tile[HALF:K])

    def wait_alleles(cb):
        @pl.when(my_t // GROUP == cb)
        def _():
            wait_bytes(ag_all.at[pl.ds(0, 2 * GROUP - 1)], ag_recv.at[cb])

        @pl.when(my_t // GROUP != cb)
        def _():
            wait_bytes(ag_all.at[pl.ds(0, 2 * GROUP)], ag_recv.at[cb])

    def wait_alleles_sent():
        wait_bytes(ag_all.at[pl.ds(0, PIECES - 1)], ag_send.at[0])

    def tile_of(t):
        return jnp.concatenate(
            [ag_all[t][:HALF], ag_all[TILES + t][:HALF], jnp.zeros((ROWS - K, LANES), F32)],
            axis=0,
        )

    def em_step(step, carry):
        phase = lax.rem(step, 3)
        parity = lax.rem(step, 2)
        follows = jnp.logical_or(phase == 1, jnp.logical_and(phase == 0, step > 0))

        def prep_p(cb):
            @pl.when(follows)
            def _():
                wait_alleles(cb)
                for t in range(cb * GROUP, (cb + 1) * GROUP):
                    p_start[t] = p_now[t]
                    p_now[t] = tile_of(t)

            p = jnp.concatenate([p_now[t] for t in range(cb * GROUP, (cb + 1) * GROUP)], axis=1)
            ph, pm, pL = split3(p)
            pad = jnp.zeros((2 * ROWS, CB), F32)
            cols = pl.ds(cb * CB, CB)
            p_rows[:, cols] = jnp.concatenate([ph, pm, ph, pm, pL, ph, pad], axis=0).astype(BF16)
            p_three[...] = jnp.concatenate([ph, pm, pL], axis=0).astype(BF16)

        def stage_a(cb, rb, slot):
            cols = pl.ds(cb * CB, CB)
            rows = pl.ds(rb * RB, RB)
            expected = dot(q_cols[rows, :], p_rows[:, cols])
            ratios = []
            for side, (counts, chance) in enumerate(
                ((alt_cnt, expected), (ref_cnt, 1.0 - expected))
            ):
                ratios.append(counts[rows, cols] * (1.0 / chance))
            ratios.append(ratios[0] - ratios[1])
            for side, ratio in enumerate(ratios):
                w_buf[slot, 2 * side] = ratio.astype(BF16)
                high = w_buf[slot, 2 * side].astype(F32)
                w_buf[slot, 2 * side + 1] = (ratio - high).astype(BF16)

        def stage_b(cb, rb, slot, sums):
            rows = pl.ds(rb * RB, RB)
            q_part = q_rows[:, rows]
            p_part = p_three[...]
            sides = []
            for side in range(2):
                high, low = w_buf[slot, 2 * side], w_buf[slot, 2 * side + 1]
                sides.append(dot(q_part, high) + dot(q_part, low))
            prop = dot_t(p_part, w_buf[slot, 4]) + dot_t(p_part, w_buf[slot, 5])
            prop_acc[:, rows] = prop if cb == 0 else prop_acc[:, rows] + prop
            return sides if sums is None else [sums[i] + sides[i] for i in range(2)]

        def send_pieces(cb, sums):
            alt, ref = [a[:ROWS] + a[ROWS : 2 * ROWS] + a[2 * ROWS :] for a in sums]
            for t in range(cb * CB // LANES, (cb + 1) * CB // LANES):
                lane = t * LANES - cb * CB
                for half in range(2):
                    piece = half * TILES + t
                    for row in range(HALF):
                        k = half * HALF + row
                        rs_send[piece, row] = jnp.concatenate(
                            [a[k : k + 1, lane : lane + LANES] for a in (alt, ref)], axis=0
                        )
                    first = ((t // 4) * 4 + t % 4) * 2 + half
                    other = ((t // 4 + 2) * 4 + (t + 2) % 4) * 2 + half
                    for target in (first, other):

                        @pl.when(s != target)
                        def _():
                            remote(
                                rs_send.at[piece],
                                rs_recv.at[parity, s],
                                rs_sems.at[2],
                                rs_sems.at[parity],
                                (target, v),
                            ).start()

        for cb in range(BLOCKS):
            prep_p(cb)
            sums = None
            stage_a(cb, 0, 0)
            stage_a(cb, 1, 1)
            for rb in range(SAMP // RB):
                if rb + 2 < SAMP // RB:
                    stage_a(cb, rb + 2, (rb + 2) % 4)
                sums = stage_b(cb, rb, rb % 4, sums)
            send_pieces(cb, sums)

        prop = prop_acc[:ROWS, :] + prop_acc[ROWS : 2 * ROWS, :] + prop_acc[2 * ROWS :, :]
        z_top[parity, v] = prop[:8]
        z_rest[parity, v] = prop[8:K]
        top_slot = z_top.at[parity, v]
        rest_slot = z_rest.at[parity, v]
        for d in (2, 1, 3):
            where = (s, along_v[d])
            remote(top_slot, top_slot, z_send.at[0], z_recv.at[parity], where).start()
            remote(rest_slot, rest_slot, z_send.at[1], y_recv.at[parity], where).start()

        def own_piece():
            wait_bytes(rs_recv.at[parity, pl.ds(0, NS - 1)], rs_sems.at[parity])
            rs_recv[parity, s] = rs_send[my_piece]
            sums = [rs_recv[parity, i] for i in range(NS)]
            while len(sums) > 1:
                sums = [sums[i] + sums[i + 1] for i in range(0, len(sums), 2)]
            alt_sum, ref_sum = sums[0][:, 0, :], sums[0][:, 1, :]
            old = pick(p_now[my_t])
            weighted = old * alt_sum
            new = clip_unit(weighted / (weighted + (1.0 - old) * ref_sum))

            @pl.when(step > 0)
            def _():
                wait_alleles_sent()

            r = old - pick(p_start[my_t])
            c = new - old - r
            squares = [jnp.sum(x * x, axis=0, keepdims=True) for x in (r, c)]
            squares = jnp.concatenate(squares, axis=0)
            ag_all[my_piece] = jnp.concatenate([new, squares, jnp.zeros((1, LANES), F32)], axis=0)
            ag_slot = ag_all.at[my_piece]
            for x, y in SERVED:
                for c in range(2):
                    if (x, y, c) != (0, 0, 0):
                        remote(
                            ag_slot, ag_slot, ag_send.at[0], ag_recv.at[my_t // GROUP], (moved(x, y, c), v)
                        ).start()

            @pl.when(phase == 1)
            def _():
                sp_out[...] = squares
                for x, y, c, d in FAR:
                    remote(
                        sp_out, sp_all.at[v, my_piece], sp_sems.at[0], sp_sems.at[1], (moved(x, y, c), along_v[d])
                    ).start()

        last_block = my_t // GROUP == BLOCKS - 1
        relaxed = jnp.logical_and(phase != 1, step < 3 * STEPS - 1)
        late = jnp.logical_and(last_block, relaxed)
        pl.when(jnp.logical_not(late))(own_piece)

        @pl.when(step == 0)
        def _():
            wait_bytes(c_all.at[pl.ds(0, NV - 1)], c_sems.at[1])
            twice_ref[...] = c_all[0] + c_all[1] + c_all[2] + c_all[3]
            wait_bytes(c_all.at[pl.ds(0, NV - 1)], c_sems.at[0])

        wait_bytes(z_top.at[parity, pl.ds(0, NV - 1)], z_recv.at[parity])
        wait_bytes(z_rest.at[parity, pl.ds(0, NV - 1)], y_recv.at[parity])
        q = q_now[...]
        top = z_top[parity, 0] + z_top[parity, 1] + z_top[parity, 2] + z_top[parity, 3]
        rest = z_rest[parity, 0] + z_rest[parity, 1] + z_rest[parity, 2] + z_rest[parity, 3]
        total = jnp.concatenate([top, rest, jnp.zeros((ROWS - K, SAMP), F32)], axis=0)
        twice = twice_ref[...]
        inner = jnp.sum(q * total, axis=0, keepdims=True)
        q_next = jnp.where(row_mask, clip_unit(q * (1.0 + (total - inner) / twice)), 0.0)

        @pl.when(phase == 1)
        def _():
            step_mix = q - q_start[...]
            curve_mix = q_next - q - step_mix
            row = [jnp.sum(a * a, axis=0, keepdims=True) for a in (step_mix, curve_mix)]
            row = jnp.concatenate(row, axis=0)
            part = row[:, :LANES]
            for t in range(1, TILES):
                part = part + row[:, t * LANES : (t + 1) * LANES]
            sq_q[s] = part

            sq_slot = sq_q.at[s]
            for x, y, c in SPREAD:
                if (x, y, c) != (0, 0, 0):
                    remote(
                        sq_slot, sq_slot, sq_sems.at[0], sq_sems.at[1], (moved(x, y, c), v)
                    ).start()

        @pl.when(phase != 1)
        def _():
            q_start[...] = q
            q_now[...] = q_next
            prep_q(q_next)

        pl.when(late)(own_piece)

        @pl.when(phase == 1)
        def _():
            for cb in range(BLOCKS):
                wait_alleles(cb)
            p_next = [tile_of(t) for t in range(TILES)]
            def alpha_of(sums):
                first = jnp.sum(sums[0:1], axis=1, keepdims=True)
                second = jnp.sum(sums[1:2], axis=1, keepdims=True)
                return jnp.maximum(1.0, jnp.sqrt(first / (second + NORM_EPS)))

            wait_bytes(sq_q.at[pl.ds(0, NS - 1)], sq_sems.at[1])
            sums = [sq_q[i] for i in range(NS)]
            while len(sums) > 1:
                sums = [sums[i] + sums[i + 1] for i in range(0, len(sums), 2)]
            alpha = alpha_of(sums[0])
            base = q_start[...]
            step_mix = q - base
            curve_mix = q_next - q - step_mix
            extra = clip_unit(base + 2.0 * alpha * step_mix + alpha * alpha * curve_mix)
            extra = jnp.where(row_mask, extra, 0.0)
            extra = extra / jnp.sum(extra, axis=0, keepdims=True)
            q_now[...] = extra
            prep_q(extra)

            for piece in range(PIECES):
                sp_all[v, piece] = ag_all[piece][HALF : HALF + 2]
            wait_bytes(sp_all.at[pl.ds(0, NV - 1)], sp_sems.at[1])
            sums = [jnp.sum(sp_all[i], axis=0) for i in range(NV)]
            alpha_p = alpha_of((sums[0] + sums[1]) + (sums[2] + sums[3]))
            for t in range(TILES):
                base_p = p_start[t]
                r = p_now[t] - base_p
                c = p_next[t] - p_now[t] - r
                extra_p = clip_unit(base_p + 2.0 * alpha_p * r + alpha_p * alpha_p * c)
                p_now[t] = jnp.where(row_mask, extra_p, 0.0)

            wait_bytes(sq_q.at[pl.ds(0, NS - 1)], sq_sems.at[0])
            wait_bytes(sp_all.at[pl.ds(0, NV - 1)], sp_sems.at[0])

        wait_bytes(z_top.at[parity, pl.ds(0, NV - 1)], z_send.at[0])
        wait_bytes(z_rest.at[parity, pl.ds(0, NV - 1)], z_send.at[1])
        wait_bytes(rs_send, rs_sems.at[2])
        wait_bytes(rs_send.at[pl.ds(0, PIECES - 1)], rs_sems.at[2])
        return carry

    lax.fori_loop(0, 3 * STEPS, em_step, 0)
    mix_ref[...] = q_now[:K, :]
    for cb in range(BLOCKS):
        wait_alleles(cb)
    for t in range(TILES):
        allele_ref[:, t * LANES : (t + 1) * LANES] = tile_of(t)[:K]
    wait_alleles_sent()


def finish(mix_in, allele_in, mix_out, allele_out):
    mix_out[...] = mix_in[...]
    allele_out[...] = allele_in[...]


def local(genotypes, observed, proportions, frequencies):
    vmem = pl.BlockSpec(memory_space=pltpu.VMEM)
    hbm = pl.BlockSpec(memory_space=pl.ANY)
    dma = pltpu.SemaphoreType.DMA
    outs = pl.pallas_call(
        kernel,
        name="em",
        out_shape=(
            jax.ShapeDtypeStruct((K, SAMP), F32),
            jax.ShapeDtypeStruct((K, VARS), F32),
        ),
        in_specs=[hbm, hbm, hbm, hbm],
        out_specs=(vmem, vmem),
        scratch_shapes=[
            pltpu.VMEM((SAMP, VARS), jnp.int32),
            pltpu.VMEM((SAMP, VARS), jnp.int32),
            pltpu.VMEM((SAMP, VARS), F32),
            pltpu.VMEM((SAMP, VARS), F32),
            pltpu.VMEM((ROWS, SAMP), F32),
            pltpu.VMEM((3 * ROWS, SAMP), F32),
            pltpu.VMEM((ROWS, SAMP), F32),
            pltpu.VMEM((ROWS, SAMP), F32),
            pltpu.VMEM((TILES, ROWS, LANES), F32),
            pltpu.VMEM((TILES, ROWS, LANES), F32),
            pltpu.VMEM((SAMP, LANES), BF16),
            pltpu.VMEM((LANES, VARS), BF16),
            pltpu.VMEM((3 * ROWS, SAMP), BF16),
            pltpu.VMEM((3 * ROWS, CB), BF16),
            pltpu.VMEM((4, 6, RB, CB), BF16),
            pltpu.VMEM((K, SAMP), F32),
            pltpu.VMEM((K, 32), F32),
            pltpu.VMEM((4, LANES), F32),
            pltpu.VMEM((NS, 4, LANES), F32),
            pltpu.VMEM((PIECES, HALF, 2, LANES), F32),
            pltpu.VMEM((2, NS, HALF, 2, LANES), F32),
            pltpu.VMEM((PIECES, 8, LANES), F32),
            pltpu.VMEM((2, NV, 8, SAMP), F32),
            pltpu.VMEM((2, NV, K - 8, SAMP), F32),
            pltpu.VMEM((NV, 1, SAMP), F32),
            pltpu.VMEM((1, SAMP), F32),
            pltpu.VMEM((NS, 2, LANES), F32),
            pltpu.VMEM((NV, PIECES, 2, LANES), F32),
            pltpu.VMEM((2, LANES), F32),
            dma((2, CHUNKS)),
            dma((2,)),
            dma((2,)),
            dma((3,)),
            dma((1,)),
            dma((BLOCKS,)),
            dma((2,)),
            dma((2,)),
            dma((2,)),
            dma((2,)),
            dma((2,)),
            dma((2,)),
        ],
        compiler_params=pltpu.CompilerParams(
            collective_id=0, has_side_effects=True, vmem_limit_bytes=60 * 1024 * 1024
        ),
    )(genotypes, observed, proportions, frequencies)
    return pl.pallas_call(
        finish,
        name="finish",
        out_shape=(
            jax.ShapeDtypeStruct((K, SAMP), F32),
            jax.ShapeDtypeStruct((K, VARS), F32),
        ),
        in_specs=[vmem, vmem],
        out_specs=(vmem, vmem),
    )(*outs)


def solution(mesh):
    placed = (P("samp", "var"), P("samp", "var"), P(None, "samp"), P(None, ("samp", "var")))
    return jax.shard_map(
        local,
        mesh=mesh,
        in_specs=placed,
        out_specs=(P(None, "samp"), P(None, "var")),
        check_vma=False,
    )
```

```python
import jax
import jax.numpy as jnp
from jax import lax
from jax.experimental import pallas as pl
from jax.experimental.pallas import tpu as pltpu
from jax.sharding import PartitionSpec as P

STEPS = 2
CLIP_LOW = 1e-05
NORM_EPS = 1e-10
MESH = pl.DeviceIdType.MESH

K = 10
ROWS = 16
NS = 32
NV = 4
SAMP = 1024
VARS = 1024
LANES = 128
TILES = VARS // LANES
HALF = K // 2
PIECES = 2 * TILES
SERVED = ((2, 0), (1, 1), (1, 3), (3, 0), (1, 0), (0, 3), (0, 1), (0, 0))
SPREAD = sorted(
    ((x, y, c) for x in range(4) for y in range(4) for c in range(2)),
    key=lambda d: -(min(d[0], 4 - d[0]) + min(d[1], 4 - d[1])),
)
RB = 256
CB = 256
BLOCKS = VARS // CB
GROUP = CB // LANES
CHUNK = 128
CHUNKS = SAMP // CHUNK

F32 = jnp.float32
BF16 = jnp.bfloat16
FAR = sorted(
    ((x, y, c, d) for x, y in SERVED for c in range(2) for d in range(1, NV)),
    key=lambda e: -sum(min(a, 4 - a) for a in (e[0], e[1], e[3])),
)


def clip_unit(values):
    return jnp.clip(values, CLIP_LOW, 1.0 - CLIP_LOW)


def split3(values):
    high = values.astype(BF16).astype(F32)
    rest = values - high
    mid = rest.astype(BF16).astype(F32)
    low = (rest - mid).astype(BF16).astype(F32)
    return high, mid, low


def dot(a, b):
    return lax.dot_general(
        a, b, (((1,), (0,)), ((), ())), preferred_element_type=F32
    )


def dot_t(a, b):
    return lax.dot_general(
        a, b, (((1,), (1,)), ((), ())), preferred_element_type=F32
    )


def kernel(
    geno_hbm,
    seen_hbm,
    props_ref,
    freqs_ref,
    mix_ref,
    allele_ref,
    geno_buf,
    seen_buf,
    alt_cnt,
    ref_cnt,
    count_acc,
    prop_acc,
    q_now,
    q_start,
    p_now,
    p_start,
    q_cols,
    p_rows,
    q_rows,
    p_three,
    w_buf,
    props_buf,
    freqs_buf,
    f_send,
    f_recv,
    rs_send,
    rs_recv,
    ag_all,
    z_top,
    z_rest,
    c_all,
    twice_ref,
    sq_q,
    sp_all,
    sp_out,
    load_sem,
    small_sem,
    f_sems,
    rs_sems,
    ag_send,
    ag_recv,
    z_send,
    z_recv,
    y_recv,
    c_sems,
    sq_sems,
    sp_sems,
):
    s = lax.axis_index("samp")
    v = lax.axis_index("var")
    chip_x = s // 8
    chip_y = lax.rem(s // 2, 4)
    core = lax.rem(s, 2)
    my_t = lax.rem(chip_x, 2) * 4 + lax.rem(chip_y + 2 * (chip_x // 2), 4)
    my_piece = core * TILES + my_t

    along_x = [lax.rem(chip_x + d, 4) * 8 for d in range(4)]
    along_y = [lax.rem(chip_y + d, 4) * 2 for d in range(4)]
    cores = (core, 1 - core)
    along_v = [lax.rem(v + d, NV) for d in range(NV)]

    def moved(x, y, c):
        return along_x[x] + along_y[y] + cores[c]

    home = s // TILES

    def remote(src, dst, send_sem, recv_sem, where):
        return pltpu.make_async_remote_copy(
            src_ref=src,
            dst_ref=dst,
            send_sem=send_sem,
            recv_sem=recv_sem,
            device_id=where,
            device_id_type=MESH,
        )

    def wait_bytes(ref, sem):
        pltpu.make_async_copy(ref, ref, sem).wait()

    def load(chunk):
        rows = pl.ds(chunk * CHUNK, CHUNK)
        return (
            pltpu.make_async_copy(geno_hbm.at[rows], geno_buf.at[rows], load_sem.at[0, chunk]),
            pltpu.make_async_copy(seen_hbm.at[rows], seen_buf.at[rows], load_sem.at[1, chunk]),
        )

    barrier = pltpu.get_barrier_semaphore()

    def greet(where):
        pl.semaphore_signal(barrier, inc=1, device_id=where, device_id_type=MESH)

    first_source = v * TILES
    for i in range(NS):
        source = (first_source + i // NV, i % NV)

        @pl.when(jnp.logical_or(source[0] != s, v != source[1]))
        def _():
            greet(source)

    for x, y, c in SPREAD:
        if (x, y, c) != (0, 0, 0):
            greet((moved(x, y, c), v))
    for d in (2, 1, 3):
        greet((s, along_v[d]))

    small = (
        pltpu.make_async_copy(freqs_ref, freqs_buf, small_sem.at[0]),
        pltpu.make_async_copy(props_ref, props_buf, small_sem.at[1]),
    )
    for copy in small:
        copy.start()
    for chunk in range(CHUNKS):
        for copy in load(chunk):
            copy.start()

    row_ids = lax.broadcasted_iota(jnp.int32, (ROWS, 1), 0)
    row_mask = row_ids < K

    small[0].wait()
    block = freqs_buf[...]
    tail = jnp.concatenate([block[8:K], jnp.zeros((12 - K, 32), F32)], axis=0)
    f_send[...] = jnp.concatenate([block[:4], block[4:8], tail, jnp.zeros((4, 32), F32)], axis=1)

    @pl.when(home == v)
    def _():
        pl.semaphore_wait(barrier, NS - 1 + NV - 1 + NS - 1)

    @pl.when(home != v)
    def _():
        pl.semaphore_wait(barrier, NS - 1 + NV - 1 + NS)

    my_slot = NV * lax.rem(s, TILES) + v

    for x, y, c in SPREAD:
        copy = remote(f_send, f_recv.at[my_slot], f_sems.at[0], f_sems.at[1], (moved(x, y, c), home))
        if (x, y, c) != (0, 0, 0):
            copy.start()
        else:
            pl.when(home != v)(copy.start)

    small[1].wait()
    q_now[...] = jnp.concatenate([props_buf[...], jnp.zeros((ROWS - K, SAMP), F32)], axis=0)

    def prep_q(q):
        qh, qm, ql = split3(q)
        q_cols[...] = jnp.concatenate([qh, qh, qm, qm, qh, ql], axis=0).T.astype(BF16)
        q_rows[...] = jnp.concatenate([qh, qm, ql], axis=0).astype(BF16)

    prep_q(q_now[...])

    count_w = jnp.full((ROWS, VARS), 2.0, BF16)

    def convert(chunk):
        for copy in load(chunk):
            copy.wait()
        rows = pl.ds(chunk * CHUNK, CHUNK)
        seen = seen_buf[rows, :].astype(F32)
        alt = seen * geno_buf[rows, :].astype(F32)
        alt_cnt[rows, :] = alt
        ref_cnt[rows, :] = 2.0 * seen - alt
        count_acc[:, rows] = dot_t(count_w, seen.astype(BF16))

    for chunk in range(CHUNKS):
        convert(chunk)

    c_all[v] = count_acc[:1, :]
    c_slot = c_all.at[v]
    for d in (2, 1, 3):
        remote(c_slot, c_slot, c_sems.at[0], c_sems.at[1], (s, along_v[d])).start()

    @pl.when(home == v)
    def _():
        wait_bytes(f_recv.at[pl.ds(0, NS - 1)], f_sems.at[1])
        f_recv[my_slot] = f_send[...]

    @pl.when(home != v)
    def _():
        wait_bytes(f_recv, f_sems.at[1])

    lane_group = lax.broadcasted_iota(jnp.int32, (4, LANES), 1) // 32
    for t in range(TILES):
        groups = []
        for group in range(3):
            rows4 = jnp.zeros((4, LANES), F32)
            for m in range(NV):
                shift = (32 * (m - group)) % LANES
                got = f_recv[NV * t + m]
                got = pltpu.roll(got, shift, 1) if shift else got
                rows4 = jnp.where(lane_group == m, got, rows4)
            groups.append(rows4)
        p_now[t] = jnp.concatenate(groups + [jnp.zeros((4, LANES), F32)], axis=0)
        p_start[t] = p_now[t]

    @pl.when(home == v)
    def _():
        wait_bytes(f_recv.at[pl.ds(0, NS - 1)], f_sems.at[0])

    @pl.when(home != v)
    def _():
        wait_bytes(f_recv, f_sems.at[0])

    def pick(tile):
        return jnp.where(core == 0, tile[:HALF], tile[HALF:K])

    def wait_alleles(cb):
        @pl.when(my_t // GROUP == cb)
        def _():
            wait_bytes(ag_all.at[pl.ds(0, 2 * GROUP - 1)], ag_recv.at[cb])

        @pl.when(my_t // GROUP != cb)
        def _():
            wait_bytes(ag_all.at[pl.ds(0, 2 * GROUP)], ag_recv.at[cb])

    def wait_alleles_sent():
        wait_bytes(ag_all.at[pl.ds(0, PIECES - 1)], ag_send.at[0])

    def tile_of(t):
        return jnp.concatenate(
            [ag_all[t][:HALF], ag_all[TILES + t][:HALF], jnp.zeros((ROWS - K, LANES), F32)],
            axis=0,
        )

    def em_step(step, carry):
        phase = lax.rem(step, 3)
        parity = lax.rem(step, 2)
        follows = jnp.logical_or(phase == 1, jnp.logical_and(phase == 0, step > 0))

        def prep_p(cb):
            @pl.when(follows)
            def _():
                wait_alleles(cb)
                for t in range(cb * GROUP, (cb + 1) * GROUP):
                    p_start[t] = p_now[t]
                    p_now[t] = tile_of(t)

            p = jnp.concatenate([p_now[t] for t in range(cb * GROUP, (cb + 1) * GROUP)], axis=1)
            ph, pm, pL = split3(p)
            cols = pl.ds(cb * CB, CB)
            p_rows[:, cols] = jnp.concatenate([ph, pm, ph, pm, pL, ph], axis=0).astype(BF16)
            p_three[...] = jnp.concatenate([ph, pm, pL], axis=0).astype(BF16)

        def stage_a(cb, rb, slot):
            cols = pl.ds(cb * CB, CB)
            rows = pl.ds(rb * RB, RB)
            expected = dot(q_cols[rows, :], p_rows[:, cols])
            ratios = []
            for side, (counts, chance) in enumerate(
                ((alt_cnt, expected), (ref_cnt, 1.0 - expected))
            ):
                ratios.append(counts[rows, cols] * (1.0 / chance))
            ratios.append(ratios[0] - ratios[1])
            for side, ratio in enumerate(ratios):
                w_buf[slot, 2 * side] = ratio.astype(BF16)
                high = w_buf[slot, 2 * side].astype(F32)
                w_buf[slot, 2 * side + 1] = (ratio - high).astype(BF16)

        def stage_b(cb, rb, slot, sums):
            rows = pl.ds(rb * RB, RB)
            q_part = q_rows[:, rows]
            p_part = p_three[...]
            sides = []
            for side in range(2):
                high, low = w_buf[slot, 2 * side], w_buf[slot, 2 * side + 1]
                sides.append(dot(q_part, high) + dot(q_part, low))
            prop = dot_t(p_part, w_buf[slot, 4]) + dot_t(p_part, w_buf[slot, 5])
            prop_acc[:, rows] = prop if cb == 0 else prop_acc[:, rows] + prop
            return sides if sums is None else [sums[i] + sides[i] for i in range(2)]

        def send_pieces(cb, sums):
            alt, ref = [a[:ROWS] + a[ROWS : 2 * ROWS] + a[2 * ROWS :] for a in sums]
            for t in range(cb * CB // LANES, (cb + 1) * CB // LANES):
                lane = t * LANES - cb * CB
                for half in range(2):
                    piece = half * TILES + t
                    for row in range(HALF):
                        k = half * HALF + row
                        rs_send[piece, row] = jnp.concatenate(
                            [a[k : k + 1, lane : lane + LANES] for a in (alt, ref)], axis=0
                        )
                    first = ((t // 4) * 4 + t % 4) * 2 + half
                    other = ((t // 4 + 2) * 4 + (t + 2) % 4) * 2 + half
                    for target in (first, other):

                        @pl.when(s != target)
                        def _():
                            remote(
                                rs_send.at[piece],
                                rs_recv.at[parity, s],
                                rs_sems.at[2],
                                rs_sems.at[parity],
                                (target, v),
                            ).start()

        for cb in range(BLOCKS):
            prep_p(cb)
            sums = None
            stage_a(cb, 0, 0)
            stage_a(cb, 1, 1)
            for rb in range(SAMP // RB):
                if rb + 2 < SAMP // RB:
                    stage_a(cb, rb + 2, (rb + 2) % 4)
                sums = stage_b(cb, rb, rb % 4, sums)
            send_pieces(cb, sums)

        prop = prop_acc[:ROWS, :] + prop_acc[ROWS : 2 * ROWS, :] + prop_acc[2 * ROWS :, :]
        z_top[parity, v] = prop[:8]
        z_rest[parity, v] = prop[8:K]
        top_slot = z_top.at[parity, v]
        rest_slot = z_rest.at[parity, v]
        for d in (2, 1, 3):
            where = (s, along_v[d])
            remote(top_slot, top_slot, z_send.at[0], z_recv.at[parity], where).start()
            remote(rest_slot, rest_slot, z_send.at[1], y_recv.at[parity], where).start()

        def own_piece():
            wait_bytes(rs_recv.at[parity, pl.ds(0, NS - 1)], rs_sems.at[parity])
            rs_recv[parity, s] = rs_send[my_piece]
            sums = [rs_recv[parity, i] for i in range(NS)]
            while len(sums) > 1:
                sums = [sums[i] + sums[i + 1] for i in range(0, len(sums), 2)]
            alt_sum, ref_sum = sums[0][:, 0, :], sums[0][:, 1, :]
            old = pick(p_now[my_t])
            weighted = old * alt_sum
            new = clip_unit(weighted / (weighted + (1.0 - old) * ref_sum))

            @pl.when(step > 0)
            def _():
                wait_alleles_sent()

            r = old - pick(p_start[my_t])
            c = new - old - r
            squares = [jnp.sum(x * x, axis=0, keepdims=True) for x in (r, c)]
            squares = jnp.concatenate(squares, axis=0)
            ag_all[my_piece] = jnp.concatenate([new, squares, jnp.zeros((1, LANES), F32)], axis=0)
            ag_slot = ag_all.at[my_piece]
            for x, y in SERVED:
                for c in range(2):
                    if (x, y, c) != (0, 0, 0):
                        remote(
                            ag_slot, ag_slot, ag_send.at[0], ag_recv.at[my_t // GROUP], (moved(x, y, c), v)
                        ).start()

            @pl.when(phase == 1)
            def _():
                sp_out[...] = squares
                for x, y, c, d in FAR:
                    remote(
                        sp_out, sp_all.at[v, my_piece], sp_sems.at[0], sp_sems.at[1], (moved(x, y, c), along_v[d])
                    ).start()

        last_block = my_t // GROUP == BLOCKS - 1
        relaxed = jnp.logical_and(phase != 1, step < 3 * STEPS - 1)
        late = jnp.logical_and(last_block, relaxed)
        pl.when(jnp.logical_not(late))(own_piece)

        @pl.when(step == 0)
        def _():
            wait_bytes(c_all.at[pl.ds(0, NV - 1)], c_sems.at[1])
            twice_ref[...] = c_all[0] + c_all[1] + c_all[2] + c_all[3]
            wait_bytes(c_all.at[pl.ds(0, NV - 1)], c_sems.at[0])

        wait_bytes(z_top.at[parity, pl.ds(0, NV - 1)], z_recv.at[parity])
        wait_bytes(z_rest.at[parity, pl.ds(0, NV - 1)], y_recv.at[parity])
        q = q_now[...]
        top = z_top[parity, 0] + z_top[parity, 1] + z_top[parity, 2] + z_top[parity, 3]
        rest = z_rest[parity, 0] + z_rest[parity, 1] + z_rest[parity, 2] + z_rest[parity, 3]
        total = jnp.concatenate([top, rest, jnp.zeros((ROWS - K, SAMP), F32)], axis=0)
        twice = twice_ref[...]
        inner = jnp.sum(q * total, axis=0, keepdims=True)
        q_next = jnp.where(row_mask, clip_unit(q * (1.0 + (total - inner) / twice)), 0.0)

        @pl.when(phase == 1)
        def _():
            step_mix = q - q_start[...]
            curve_mix = q_next - q - step_mix
            row = [jnp.sum(a * a, axis=0, keepdims=True) for a in (step_mix, curve_mix)]
            row = jnp.concatenate(row, axis=0)
            part = row[:, :LANES]
            for t in range(1, TILES):
                part = part + row[:, t * LANES : (t + 1) * LANES]
            sq_q[s] = part

            sq_slot = sq_q.at[s]
            for x, y, c in SPREAD:
                if (x, y, c) != (0, 0, 0):
                    remote(
                        sq_slot, sq_slot, sq_sems.at[0], sq_sems.at[1], (moved(x, y, c), v)
                    ).start()

        @pl.when(phase != 1)
        def _():
            q_start[...] = q
            q_now[...] = q_next
            prep_q(q_next)

        pl.when(late)(own_piece)

        @pl.when(phase == 1)
        def _():
            for cb in range(BLOCKS):
                wait_alleles(cb)
            p_next = [tile_of(t) for t in range(TILES)]
            def alpha_of(sums):
                first = jnp.sum(sums[0:1], axis=1, keepdims=True)
                second = jnp.sum(sums[1:2], axis=1, keepdims=True)
                return jnp.maximum(1.0, jnp.sqrt(first / (second + NORM_EPS)))

            wait_bytes(sq_q.at[pl.ds(0, NS - 1)], sq_sems.at[1])
            sums = [sq_q[i] for i in range(NS)]
            while len(sums) > 1:
                sums = [sums[i] + sums[i + 1] for i in range(0, len(sums), 2)]
            alpha = alpha_of(sums[0])
            base = q_start[...]
            step_mix = q - base
            curve_mix = q_next - q - step_mix
            extra = clip_unit(base + 2.0 * alpha * step_mix + alpha * alpha * curve_mix)
            extra = jnp.where(row_mask, extra, 0.0)
            extra = extra / jnp.sum(extra, axis=0, keepdims=True)
            q_now[...] = extra
            prep_q(extra)

            for piece in range(PIECES):
                sp_all[v, piece] = ag_all[piece][HALF : HALF + 2]
            wait_bytes(sp_all.at[pl.ds(0, NV - 1)], sp_sems.at[1])
            sums = [jnp.sum(sp_all[i], axis=0) for i in range(NV)]
            alpha_p = alpha_of((sums[0] + sums[1]) + (sums[2] + sums[3]))
            for t in range(TILES):
                base_p = p_start[t]
                r = p_now[t] - base_p
                c = p_next[t] - p_now[t] - r
                extra_p = clip_unit(base_p + 2.0 * alpha_p * r + alpha_p * alpha_p * c)
                p_now[t] = jnp.where(row_mask, extra_p, 0.0)

            wait_bytes(sq_q.at[pl.ds(0, NS - 1)], sq_sems.at[0])
            wait_bytes(sp_all.at[pl.ds(0, NV - 1)], sp_sems.at[0])

        wait_bytes(z_top.at[parity, pl.ds(0, NV - 1)], z_send.at[0])
        wait_bytes(z_rest.at[parity, pl.ds(0, NV - 1)], z_send.at[1])
        wait_bytes(rs_send, rs_sems.at[2])
        wait_bytes(rs_send.at[pl.ds(0, PIECES - 1)], rs_sems.at[2])
        return carry

    lax.fori_loop(0, 3 * STEPS, em_step, 0)
    mix_ref[...] = q_now[:K, :]
    for cb in range(BLOCKS):
        wait_alleles(cb)
    for t in range(TILES):
        allele_ref[:, t * LANES : (t + 1) * LANES] = tile_of(t)[:K]
    wait_alleles_sent()


def finish(mix_in, allele_in, mix_out, allele_out):
    mix_out[...] = mix_in[...]
    allele_out[...] = allele_in[...]


def local(genotypes, observed, proportions, frequencies):
    vmem = pl.BlockSpec(memory_space=pltpu.VMEM)
    hbm = pl.BlockSpec(memory_space=pl.ANY)
    dma = pltpu.SemaphoreType.DMA
    outs = pl.pallas_call(
        kernel,
        name="em",
        out_shape=(
            jax.ShapeDtypeStruct((K, SAMP), F32),
            jax.ShapeDtypeStruct((K, VARS), F32),
        ),
        in_specs=[hbm, hbm, hbm, hbm],
        out_specs=(vmem, vmem),
        scratch_shapes=[
            pltpu.VMEM((SAMP, VARS), jnp.int32),
            pltpu.VMEM((SAMP, VARS), jnp.int32),
            pltpu.VMEM((SAMP, VARS), F32),
            pltpu.VMEM((SAMP, VARS), F32),
            pltpu.VMEM((ROWS, SAMP), F32),
            pltpu.VMEM((3 * ROWS, SAMP), F32),
            pltpu.VMEM((ROWS, SAMP), F32),
            pltpu.VMEM((ROWS, SAMP), F32),
            pltpu.VMEM((TILES, ROWS, LANES), F32),
            pltpu.VMEM((TILES, ROWS, LANES), F32),
            pltpu.VMEM((SAMP, 6 * ROWS), BF16),
            pltpu.VMEM((6 * ROWS, VARS), BF16),
            pltpu.VMEM((3 * ROWS, SAMP), BF16),
            pltpu.VMEM((3 * ROWS, CB), BF16),
            pltpu.VMEM((4, 6, RB, CB), BF16),
            pltpu.VMEM((K, SAMP), F32),
            pltpu.VMEM((K, 32), F32),
            pltpu.VMEM((4, LANES), F32),
            pltpu.VMEM((NS, 4, LANES), F32),
            pltpu.VMEM((PIECES, HALF, 2, LANES), F32),
            pltpu.VMEM((2, NS, HALF, 2, LANES), F32),
            pltpu.VMEM((PIECES, 8, LANES), F32),
            pltpu.VMEM((2, NV, 8, SAMP), F32),
            pltpu.VMEM((2, NV, K - 8, SAMP), F32),
            pltpu.VMEM((NV, 1, SAMP), F32),
            pltpu.VMEM((1, SAMP), F32),
            pltpu.VMEM((NS, 2, LANES), F32),
            pltpu.VMEM((NV, PIECES, 2, LANES), F32),
            pltpu.VMEM((2, LANES), F32),
            dma((2, CHUNKS)),
            dma((2,)),
            dma((2,)),
            dma((3,)),
            dma((1,)),
            dma((BLOCKS,)),
            dma((2,)),
            dma((2,)),
            dma((2,)),
            dma((2,)),
            dma((2,)),
            dma((2,)),
        ],
        compiler_params=pltpu.CompilerParams(
            collective_id=0, has_side_effects=True, vmem_limit_bytes=60 * 1024 * 1024
        ),
    )(genotypes, observed, proportions, frequencies)
    return pl.pallas_call(
        finish,
        name="finish",
        out_shape=(
            jax.ShapeDtypeStruct((K, SAMP), F32),
            jax.ShapeDtypeStruct((K, VARS), F32),
        ),
        in_specs=[vmem, vmem],
        out_specs=(vmem, vmem),
    )(*outs)


def solution(mesh):
    placed = (P("samp", "var"), P("samp", "var"), P(None, "samp"), P(None, ("samp", "var")))
    return jax.shard_map(
        local,
        mesh=mesh,
        in_specs=placed,
        out_specs=(P(None, "samp"), P(None, "var")),
        check_vma=False,
    )
```
